128 devices in a mesh: rows: 16 (over x, z), cols: 8 (over y, core).
Axes of the slice: x: 4, y: 4, z: 4, core: 2. Of those that a mesh axis runs over, the one named last changes fastest.
Arguments:
- band: float32 [16, 8, 1024, 1024], P('rows', 'cols'), may hold values from -6 to 6
- diag: float32 [8, 1024, 1024], P('cols', 'rows'), as said below
- row_factors: bfloat16 [16, 8, 2, 1024, 256], P('rows', 'cols'), as said below
- row_ranks: int32 [16, 8], P('rows', 'cols'), may hold values from 32 to 256
- col_factors: bfloat16 [8, 8, 2, 1024, 256], P(None, 'cols', None, 'rows'), as said below
- col_ranks: int32 [8, 8], replicated, may hold values from 32 to 256
Outputs:
- band_out: float32 [16, 8, 1024, 1024], P('rows', 'cols')
- diag_out: float32 [8, 1024, 1024], P('cols', 'rows')
The draws below stay inside these ranges and needn't reach their ends.
Inputs may be any that keep to these rules, and one draw needn't show every extreme that they name: `diag`: every new_diag[c] is symmetric positive definite. `row_factors`: columns of a factor beyond its rank hold arbitrary values. `col_factors`: columns of a factor beyond its rank hold arbitrary values.
All inputs are finite; a program needn't handle non-finite values.
Results may differ from the reference program's by a relative error of at most 0.002.
Values may be sent and summed in bfloat16 or wider, within the bound.
No kernel may reach another device: no remote copies, remote signals or barrier semaphores. Data moves between devices by JAX's collectives and lax.ppermute only.
A program may use at most 128 MiB of HBM per device.

```python
import math
import jax
import jax.numpy as jnp
from jax import lax

TILE = 1024
RANK = 256
TILE_ROWS = 16
BAND_COLS = 8
PANELS = 8


def rank_law(key, row_count):
    level_key, extra_key = jax.random.split(key)
    levels = jax.random.randint(level_key, (row_count, 1), 0, 4)
    extras = jax.random.randint(extra_key, (row_count, PANELS), 0, RANK // 4)
    return jnp.minimum(RANK // 8 + levels * (RANK // 4) + extras, RANK).astype(jnp.int32)


def factor_law(key, row_count):
    base_key, side_key = jax.random.split(key)
    bases = 0.2 * jax.random.normal(base_key, (row_count, PANELS, 1, TILE, RANK), jnp.float32)
    side_part = jax.random.normal(side_key, (row_count, PANELS, 1, TILE, RANK), jnp.float32) / math.sqrt(TILE)
    return jnp.concatenate([bases, side_part], axis=2).astype(jnp.bfloat16)


def draw_row_factors(key, part):
    return factor_law(jax.random.fold_in(key, 22), TILE_ROWS)


def draw_row_ranks(key, part):
    return rank_law(jax.random.fold_in(key, 21), TILE_ROWS)


def draw_col_factors(key, part):
    return factor_law(jax.random.fold_in(key, 12), BAND_COLS)


def draw_col_ranks(key, part):
    return rank_law(jax.random.fold_in(key, 11), BAND_COLS)


def draw_diag(key, part):
    factors = draw_col_factors(key, part).astype(jnp.float32)
    rank_list = draw_col_ranks(key, part)
    positions = jnp.arange(RANK, dtype=jnp.int32)
    spread_key = jax.random.fold_in(key, 13)
    coherent_key = jax.random.fold_in(key, 14)

    def one_diag(tile_col):
        col_part = factors[tile_col]
        own_ranks = rank_list[tile_col]
        kept_mask = (positions[None, :, None] < own_ranks[:, None, None]) & (positions[None, None, :] < own_ranks[:, None, None])
        pair_core = jnp.where(kept_mask, jnp.einsum('kxa,kxb->kab', col_part[:, 1], col_part[:, 1], precision=lax.Precision.HIGHEST), 0.0)
        left_part = jnp.einsum('kxa,kab->kxb', col_part[:, 0], pair_core, precision=lax.Precision.HIGHEST)
        summed = jnp.einsum('kxb,kyb->xy', left_part, col_part[:, 0], precision=lax.Precision.HIGHEST)
        noise_draw = jax.random.normal(jax.random.fold_in(spread_key, tile_col), (TILE, TILE), jnp.float32)
        coherent = jax.random.normal(jax.random.fold_in(coherent_key, tile_col), (TILE, 8), jnp.float32)
        spread = jnp.dot(noise_draw, noise_draw.T, precision=lax.Precision.HIGHEST) / TILE + 4.0 * jnp.eye(TILE, dtype=jnp.float32)
        spread = spread + jnp.dot(coherent, coherent.T, precision=lax.Precision.HIGHEST) / 16.0
        return summed + spread
    return lax.map(one_diag, jnp.arange(BAND_COLS, dtype=jnp.int32))


def level_of(own_key, extent, cuts, low, high):
    level = 1.0
    for axis_at, shards_of in cuts:
        steps = jax.random.uniform(jax.random.fold_in(jax.random.fold_in(own_key, 6), axis_at), (shards_of,), jnp.float32, low / len(cuts), high / len(cuts))
        level = level * jnp.repeat(jnp.exp(steps), extent[axis_at] // shards_of).reshape((-1,) + (1,) * (len(extent) - 1 - axis_at))
    return level


def scatter_about(stream_key, dims, deviation, reach, shards=(), kind=jnp.bfloat16):
    array = jax.random.normal(stream_key, dims, jnp.float32) * deviation
    if len(shards) > 0:
        array = level_of(stream_key, dims, shards, -0.22, 0.18) * array
    return jnp.clip(array, min=-reach, max=reach).astype(kind)


def setup_inputs(seed: int = 0) -> dict:
    streams_of = jax.random.split(jax.random.key(seed), 7)
    return {
        "band": scatter_about(streams_of[0], (TILE_ROWS, BAND_COLS, TILE, TILE), 1.0, 6.0, ((0, 16), (1, 8)), jnp.float32),
        "diag": draw_diag(jax.random.fold_in(streams_of[6], 71), 0),
        "row_factors": draw_row_factors(jax.random.fold_in(streams_of[6], 71), 0),
        "row_ranks": draw_row_ranks(jax.random.fold_in(streams_of[6], 71), 0),
        "col_factors": draw_col_factors(jax.random.fold_in(streams_of[6], 71), 0),
        "col_ranks": draw_col_ranks(jax.random.fold_in(streams_of[6], 71), 0),
    }


def masked_core(side_row, rank_row, side_col, rank_col):
    pair_core = jnp.einsum('kxa,kxb->kab', side_row.astype(jnp.float32), side_col.astype(jnp.float32), precision=lax.Precision.HIGHEST)
    positions = jnp.arange(side_row.shape[2], dtype=jnp.int32)
    kept_mask = (positions[None, :, None] < rank_row[:, None, None]) & (positions[None, None, :] < rank_col[:, None, None])
    return jnp.where(kept_mask, pair_core, 0.0).astype(jnp.bfloat16)

def pair_sum(base_row, side_row, rank_row, base_col, side_col, rank_col):
    pair_core = masked_core(side_row, rank_row, side_col, rank_col)
    left_part = jnp.einsum('kxa,kab->kxb', base_row.astype(jnp.float32), pair_core.astype(jnp.float32), precision=lax.Precision.HIGHEST).astype(jnp.bfloat16)
    return jnp.einsum('kxb,kyb->xy', left_part.astype(jnp.float32), base_col.astype(jnp.float32), precision=lax.Precision.HIGHEST)

def reference(band, diag, row_factors, row_ranks, col_factors, col_ranks):

    def one_row(tile_row):
        row_part = row_factors[tile_row]
        row_rank = row_ranks[tile_row]

        def one_tile(tile_col):
            col_part = col_factors[tile_col]
            return band[tile_row, tile_col] - pair_sum(row_part[:, 0], row_part[:, 1], row_rank, col_part[:, 0], col_part[:, 1], col_ranks[tile_col])
        return lax.map(one_tile, jnp.arange(BAND_COLS, dtype=jnp.int32))
    updated = lax.map(one_row, jnp.arange(TILE_ROWS, dtype=jnp.int32))

    def one_diag(tile_col):
        col_part = col_factors[tile_col]
        return diag[tile_col] - pair_sum(col_part[:, 0], col_part[:, 1], col_ranks[tile_col], col_part[:, 0], col_part[:, 1], col_ranks[tile_col])
    new_diag = lax.map(one_diag, jnp.arange(BAND_COLS, dtype=jnp.int32))
    factor = jnp.linalg.cholesky(new_diag[0])

    def solve_tile(tile_data):
        return jax.scipy.linalg.solve_triangular(factor, tile_data.T, lower=True).T
    panel = lax.map(solve_tile, updated[:, 0])
    band_out = updated.at[:, 0].set(panel)
    diag_out = new_diag.at[0].set(factor)
    return (band_out, diag_out)
```

```python
import jax
import jax.numpy as jnp
from jax import lax
from jax.experimental import pallas as pl
from jax.experimental.pallas import tpu as pltpu
from jax.sharding import PartitionSpec as P

NB = 128
G = 8

def split2(x):
    hi = x.astype(jnp.bfloat16)
    lo = (x - hi.astype(jnp.float32)).astype(jnp.bfloat16)
    return hi, lo

def nt(a, b):
    return lax.dot_general(a, b, (((1,), (1,)), ((), ())), preferred_element_type=jnp.float32)

def nt3(ah, al, bh, bl):
    return nt(jnp.concatenate([ah, al, ah], axis=1), jnp.concatenate([bh, bh, bl], axis=1))

def factor_block(t_ref):
    for g in range(NB // G):
        v = t_ref[g * G:(g + 1) * G, :]
        cols = [jnp.broadcast_to(v[:, g * G + j:g * G + j + 1], (G, NB)) for j in range(G)]
        b = [[jnp.broadcast_to(cols[j][s:s + 1, :], (G, NB)) if s >= j else None for j in range(G)] for s in range(G)]
        low = [[None] * G for _ in range(G)]
        rinv = [None] * G
        r = [jnp.broadcast_to(v[s:s + 1, :], (G, 2 * NB)) for s in range(G)]
        two = lambda x: jnp.concatenate([x, x], axis=1)
        for j in range(G):
            rinv[j] = lax.rsqrt(b[j][j])
            for s in range(j + 1, G):
                low[s][j] = b[s][j] * rinv[j]
            for t in range(j + 1, G):
                for s in range(t, G):
                    b[s][t] = b[s][t] - low[s][j] * low[t][j]
            r[j] = r[j] * two(rinv[j])
            for s in range(j + 1, G):
                r[s] = r[s] - two(low[s][j]) * r[j]
        m = [None] * G
        for s in reversed(range(G)):
            acc = r[s]
            for t in range(s + 1, G):
                acc = acc - two(low[t][s]) * m[t]
            m[s] = acc * two(rinv[s])
        sub = lax.broadcasted_iota(jnp.int32, (G, 2 * NB), 0)
        out = r[0]
        for s in range(1, G):
            out = jnp.where(sub == s, r[s], out)
        t_ref[g * G:(g + 1) * G, :] = out
        for rb in range(g + 1, NB // G):
            w = t_ref[rb * G:(rb + 1) * G, :]
            acc = w
            for j in range(G):
                wc = jnp.broadcast_to(w[:, g * G + j:g * G + j + 1], (G, NB))
                acc = acc - two(wc) * m[j]
            t_ref[rb * G:(rb + 1) * G, :] = acc

def chol_body(a_ref, inv_ref, t_ref, ph_ref, pl_ref):
    n = a_ref.shape[0]
    nblk = n // NB
    ri = lax.broadcasted_iota(jnp.int32, (NB, NB), 0)
    ci = lax.broadcasted_iota(jnp.int32, (NB, NB), 1)

    def step(j, _):
        o = pl.multiple_of(j * NB, NB)
        t_ref[:, :NB] = a_ref[pl.ds(o, NB), pl.ds(o, NB)]
        t_ref[:, NB:] = jnp.where(ri == ci, 1.0, 0.0)
        factor_block(t_ref)
        inv = t_ref[:, NB:]
        inv_ref[pl.ds(o, NB), :] = inv
        low = jnp.where(ri >= ci, t_ref[:, :NB].T, 0.0)
        ih, il = split2(inv)
        for v in range(nblk // 2):
            lo_row = 2 * NB * v
            @pl.when((j + 1) // 2 == v)
            def _():
                p = a_ref[lo_row:, pl.ds(o, NB)]
                ph, plo = split2(p)
                x = nt3(ph, plo, ih, il)
                rows = lax.broadcasted_iota(jnp.int32, x.shape, 0) + lo_row
                x = jnp.where(rows >= o + NB, x, 0.0)
                a_ref[lo_row:, pl.ds(o, NB)] = x
                xh, xl = split2(x)
                c = nt3(xh, xl, xh, xl)
                a_ref[lo_row:, lo_row:] = a_ref[lo_row:, lo_row:] - c
        a_ref[pl.ds(o, NB), pl.ds(o, NB)] = low
        return 0
    lax.fori_loop(0, nblk, step, 0)

def solve_body(b_ref, l_ref, inv_ref, x_ref, xh_ref, xl_ref):
    n = b_ref.shape[0]
    for j in range(n // NB):
        s = slice(j * NB, (j + 1) * NB)
        ih, il = split2(inv_ref[s, :])
        acc = b_ref[:, s]
        if j:
            lh, ll = split2(l_ref[s, :j * NB])
            acc = acc - nt(xh_ref[:, :j * NB], lh) - nt(xl_ref[:, :j * NB], lh) - nt(xh_ref[:, :j * NB], ll)
        ah, al = split2(acc)
        x = nt3(ah, al, ih, il)
        x_ref[:, s] = x
        xh, xl = split2(x)
        xh_ref[:, s] = xh
        xl_ref[:, s] = xl

def chol_kernel(d_ref, l_ref, inv_ref, t_ref):
    n = l_ref.shape[0]
    for i in range(n // NB):
        si = slice(i * NB, (i + 1) * NB)
        for j in range(i + 1):
            sj = slice(j * NB, (j + 1) * NB)
            l_ref[si, sj] = (d_ref[si, sj] + d_ref[sj, si].T) * 0.5
    chol_body(l_ref, inv_ref, t_ref, None, None)
    for j in range(n // NB):
        if j + 1 < n // NB:
            l_ref[j * NB:(j + 1) * NB, (j + 1) * NB:] = jnp.zeros((NB, n - (j + 1) * NB), jnp.float32)

def chol(d):
    n = d.shape[0]
    return pl.pallas_call(chol_kernel,
        out_shape=(jax.ShapeDtypeStruct((n, n), jnp.float32), jax.ShapeDtypeStruct((n, NB), jnp.float32)),
        scratch_shapes=[pltpu.VMEM((NB, 2 * NB), jnp.float32)],
        compiler_params=pltpu.CompilerParams(vmem_limit_bytes=60 << 20), name="chol")(d)

def solve(b, l, inv):
    n = b.shape[0]
    return pl.pallas_call(solve_body, out_shape=jax.ShapeDtypeStruct(b.shape, jnp.float32),
        scratch_shapes=[pltpu.VMEM((n, n), jnp.bfloat16)] * 2,
        compiler_params=pltpu.CompilerParams(vmem_limit_bytes=60 << 20), name="solve")(b, l, inv)


def core_of(side_row, rank_row, side_col, rank_col):
    pair_core = lax.dot_general(
        side_row, side_col, (((0,), (0,)), ((), ())), preferred_element_type=jnp.float32
    )
    row_positions = jnp.arange(side_row.shape[1], dtype=jnp.int32)
    col_positions = jnp.arange(side_col.shape[1], dtype=jnp.int32)
    kept_mask = (row_positions[:, None] < rank_row) & (col_positions[None, :] < rank_col)
    return jnp.where(kept_mask, pair_core, 0.0).astype(jnp.bfloat16)


def weighted(base_row, side_row, rank_row, side_col, rank_col):
    pair_core = core_of(side_row, rank_row, side_col, rank_col)
    return jnp.dot(base_row, pair_core, preferred_element_type=jnp.float32).astype(jnp.bfloat16)


def finish(left_part, base_col):
    return lax.dot_general(
        left_part, base_col, (((1,), (1,)), ((), ())), preferred_element_type=jnp.float32
    )


def pair_weighted(base_row, side_row, rank_row, side_col, rank_col):
    return weighted(base_row, side_row, rank_row, side_col, rank_col)


def pair_tile(base_row, side_row, rank_row, base_col, side_col, rank_col):
    return finish(weighted(base_row, side_row, rank_row, side_col, rank_col), base_col)


def shards(band, diag, row_factors, row_ranks, col_factors, col_ranks):
    column = lax.axis_index("cols")
    slab_idx = lax.axis_index("rows")
    slab_rows = diag.shape[1]
    own_ranks = lax.dynamic_index_in_dim(col_ranks, column, 0, keepdims=False)
    own_column = lax.all_to_all(col_factors, "cols", split_axis=0, concat_axis=1, tiled=True)
    full_column = lax.all_gather(own_column, "rows", axis=3, tiled=True)
    base_full = full_column[0, :, 0]
    side_full = full_column[0, :, 1]
    base_slab = own_column[0, :, 0]
    factors = lax.all_gather(row_factors, "cols", axis=1, tiled=True)
    piece_ranks = lax.all_gather(row_ranks, "cols", axis=1, tiled=True)

    row_pos = jnp.arange(factors.shape[-1], dtype=jnp.int32)
    rows0 = factors[0]
    core = jnp.einsum("kxa,kxb->kab", rows0[:, 1], side_full, preferred_element_type=jnp.float32)
    kept = (row_pos[None, :, None] < piece_ranks[0][:, None, None]) & (row_pos[None, None, :] < own_ranks[:, None, None])
    core = jnp.where(kept, core, 0.0).astype(jnp.bfloat16)
    left = jnp.einsum("kxa,kab->kxb", rows0[:, 0], core, preferred_element_type=jnp.float32).astype(jnp.bfloat16)
    update = jnp.einsum("kxb,kyb->xy", left, base_full, preferred_element_type=jnp.float32)[None]

    def diag_left(panel_idx):
        side_col = lax.dynamic_index_in_dim(side_full, panel_idx, 0, keepdims=False)
        base_row = lax.dynamic_index_in_dim(base_slab, panel_idx, 0, keepdims=False)
        rank_col = lax.dynamic_index_in_dim(own_ranks, panel_idx, 0, keepdims=False)
        return pair_weighted(base_row, side_col, rank_col, side_col, rank_col)

    diag_parts = lax.map(diag_left, jnp.arange(base_full.shape[0], dtype=jnp.int32))
    diag_term = jnp.einsum("kxr,kyr->xy", diag_parts, base_full, preferred_element_type=jnp.float32)
    updated = band[:, 0] - update
    new_slab = diag[0] - diag_term
    whole_diag = lax.all_gather(new_slab, "rows", axis=0, tiled=True)
    factor, inverses = chol(whole_diag)
    solved = solve(updated[0], factor, inverses)[None]
    is_first = column == 0
    band_out = jnp.where(is_first, solved, updated)[:, None]
    factor_slab = lax.dynamic_slice_in_dim(factor, slab_idx * slab_rows, slab_rows, 0)
    diag_out = jnp.where(is_first, factor_slab, new_slab)[None]
    return (band_out, diag_out)


def solution(mesh):
    placed = (
        P("rows", "cols", None, None),
        P("cols", "rows", None),
        P("rows", "cols", None, None, None),
        P("rows", "cols"),
        P(None, "cols", None, "rows", None),
        P(),
    )
    return jax.shard_map(
        shards,
        mesh=mesh,
        in_specs=placed,
        out_specs=(P("rows", "cols", None, None), P("cols", "rows", None)),
        check_vma=False,
    )
```

```python
import jax
import jax.numpy as jnp
from jax import lax
from jax.experimental import pallas as pl
from jax.experimental.pallas import tpu as pltpu
from jax.sharding import PartitionSpec as P

NB = 128
G = 8
SIDE = 4
AXES = ("rows", "cols")


def split2(x):
    hi = x.astype(jnp.bfloat16)
    lo = (x - hi.astype(jnp.float32)).astype(jnp.bfloat16)
    return hi, lo

def nt(a, b):
    return lax.dot_general(a, b, (((1,), (1,)), ((), ())), preferred_element_type=jnp.float32)

def nt3(ah, al, bh, bl):
    return nt(jnp.concatenate([ah, al, ah], axis=1), jnp.concatenate([bh, bh, bl], axis=1))

def factor_block(t_ref):
    for g in range(NB // G):
        v = t_ref[g * G:(g + 1) * G, :]
        cols = [jnp.broadcast_to(v[:, g * G + j:g * G + j + 1], (G, NB)) for j in range(G)]
        b = [[jnp.broadcast_to(cols[j][s:s + 1, :], (G, NB)) if s >= j else None for j in range(G)] for s in range(G)]
        low = [[None] * G for _ in range(G)]
        rinv = [None] * G
        r = [jnp.broadcast_to(v[s:s + 1, :], (G, 2 * NB)) for s in range(G)]
        two = lambda x: jnp.concatenate([x, x], axis=1)
        for j in range(G):
            rinv[j] = lax.rsqrt(b[j][j])
            for s in range(j + 1, G):
                low[s][j] = b[s][j] * rinv[j]
            for t in range(j + 1, G):
                for s in range(t, G):
                    b[s][t] = b[s][t] - low[s][j] * low[t][j]
            r[j] = r[j] * two(rinv[j])
            for s in range(j + 1, G):
                r[s] = r[s] - two(low[s][j]) * r[j]
        m = [None] * G
        for s in reversed(range(G)):
            acc = r[s]
            for t in range(s + 1, G):
                acc = acc - two(low[t][s]) * m[t]
            m[s] = acc * two(rinv[s])
        sub = lax.broadcasted_iota(jnp.int32, (G, 2 * NB), 0)
        out = r[0]
        for s in range(1, G):
            out = jnp.where(sub == s, r[s], out)
        t_ref[g * G:(g + 1) * G, :] = out
        for rb in range(g + 1, NB // G):
            w = t_ref[rb * G:(rb + 1) * G, :]
            acc = w
            for j in range(G):
                wc = jnp.broadcast_to(w[:, g * G + j:g * G + j + 1], (G, NB))
                acc = acc - two(wc) * m[j]
            t_ref[rb * G:(rb + 1) * G, :] = acc

def chol_body(a_ref, inv_ref, t_ref, ph_ref, pl_ref):
    n = a_ref.shape[0]
    nblk = n // NB
    ri = lax.broadcasted_iota(jnp.int32, (NB, NB), 0)
    ci = lax.broadcasted_iota(jnp.int32, (NB, NB), 1)

    def step(j, _):
        o = pl.multiple_of(j * NB, NB)
        t_ref[:, :NB] = a_ref[pl.ds(o, NB), pl.ds(o, NB)]
        t_ref[:, NB:] = jnp.where(ri == ci, 1.0, 0.0)
        factor_block(t_ref)
        inv = t_ref[:, NB:]
        inv_ref[pl.ds(o, NB), :] = inv
        low = jnp.where(ri >= ci, t_ref[:, :NB].T, 0.0)
        ih, il = split2(inv)
        for v in range(nblk // 2):
            lo_row = 2 * NB * v
            @pl.when((j + 1) // 2 == v)
            def _():
                p = a_ref[lo_row:, pl.ds(o, NB)]
                ph, plo = split2(p)
                x = nt3(ph, plo, ih, il)
                rows = lax.broadcasted_iota(jnp.int32, x.shape, 0) + lo_row
                x = jnp.where(rows >= o + NB, x, 0.0)
                a_ref[lo_row:, pl.ds(o, NB)] = x
                xh, xl = split2(x)
                c = nt3(xh, xl, xh, xl)
                a_ref[lo_row:, lo_row:] = a_ref[lo_row:, lo_row:] - c
        a_ref[pl.ds(o, NB), pl.ds(o, NB)] = low
        return 0
    lax.fori_loop(0, nblk, step, 0)

def solve_body(b_ref, l_ref, inv_ref, x_ref, xh_ref, xl_ref):
    n = b_ref.shape[0]
    for j in range(n // NB):
        s = slice(j * NB, (j + 1) * NB)
        ih, il = split2(inv_ref[s, :])
        acc = b_ref[:, s]
        if j:
            lh, ll = split2(l_ref[s, :j * NB])
            acc = acc - nt(xh_ref[:, :j * NB], lh) - nt(xl_ref[:, :j * NB], lh) - nt(xh_ref[:, :j * NB], ll)
        ah, al = split2(acc)
        x = nt3(ah, al, ih, il)
        x_ref[:, s] = x
        xh, xl = split2(x)
        xh_ref[:, s] = xh
        xl_ref[:, s] = xl


def tn(a, b):
    return lax.dot_general(a, b, (((0,), (0,)), ((), ())), preferred_element_type=jnp.float32)


def masked(core, rank):
    kept = lax.broadcasted_iota(jnp.int32, core.shape, 1) < rank
    return jnp.where(kept, core, 0.0)


def run_copies(pairs, sems, first=0):
    copies = [pltpu.make_async_copy(src, dst, sems.at[first + n]) for n, (src, dst) in enumerate(pairs)]
    for copy in copies:
        copy.start()
    return copies


def slab_copies(meta, fs, gs, u_ref, v_ref, hi_ref, lo_ref):
    x, z = meta[1], meta[2]
    panels = u_ref.shape[0]
    pairs = []
    for e in range(SIDE):
        for d in range(SIDE):
            slab = ((x + SIDE - d) % SIDE) * SIDE + (z + SIDE - e) % SIDE
            at = pl.ds(pl.multiple_of(slab * 64, 64), 64)
            pairs.append((fs[e].at[d, pl.ds(0, panels)], v_ref.at[:, at, :]))
            pairs.append((gs[d].at[e, pl.ds(0, panels)], u_ref.at[:, at, :]))
            if hi_ref is not None:
                pairs.append((fs[e].at[d, pl.ds(panels, 4)], hi_ref.at[:, at, :]))
                pairs.append((gs[d].at[e, pl.ds(panels, 4)], lo_ref.at[:, at, :]))
    return pairs


def factor_kernel(meta, *refs):
    fs, gs = refs[0:4], refs[4:8]
    l_ref, inv_ref, u_ref, v_ref, hi_ref, lo_ref, acc_ref, t_ref, sems = refs[8:]
    n = l_ref.shape[0]

    @pl.when(meta[0] == 0)
    def _():
        for copy in run_copies(slab_copies(meta, fs, gs, u_ref, v_ref, hi_ref, lo_ref), sems):
            copy.wait()
        for q in range(4):
            acc_ref[:, q * 256:(q + 1) * 256] = hi_ref[q].astype(jnp.float32) + lo_ref[q].astype(jnp.float32)

        def panel(k, _):
            rank = meta[4 + k]
            vk, uk = v_ref[k], u_ref[k]
            vk = masked(vk.astype(jnp.float32), rank).astype(jnp.bfloat16)
            core = tn(vk, vk).astype(jnp.bfloat16)
            left = jnp.dot(uk, core, preferred_element_type=jnp.float32).astype(jnp.bfloat16)
            for s in range(0, n, 256):
                acc_ref[s:s + 256, :] = acc_ref[s:s + 256, :] - nt(left[s:s + 256], uk)
            return 0
        lax.fori_loop(0, u_ref.shape[0], panel, 0)
        for i in range(n // NB):
            si = slice(i * NB, (i + 1) * NB)
            for j in range(i + 1):
                sj = slice(j * NB, (j + 1) * NB)
                l_ref[si, sj] = (acc_ref[si, sj] + acc_ref[sj, si].T) * 0.5
        chol_body(l_ref, inv_ref, t_ref, None, None)
        for j in range(n // NB - 1):
            l_ref[j * NB:(j + 1) * NB, (j + 1) * NB:] = jnp.zeros((NB, n - (j + 1) * NB), jnp.float32)


def tile_kernel(meta, *refs):
    even, odd, rows = refs[0:8], refs[8:16], refs[16:24]
    band_ref, diag_ref, l_hbm, inv_hbm, out_ref, dout_ref = refs[24:30]
    u_ref, v_ref, ru_ref, rv_ref, l_ref, inv_ref, xh_ref, xl_ref, sems = refs[30:]
    n = out_ref.shape[0]
    panels = u_ref.shape[0]
    column, slab = meta[0], meta[3]
    y, core_at = column // 2, column % 2
    at = pl.ds(pl.multiple_of(slab * 64, 64), 64)

    copies = []
    for e in range(SIDE):
        near = ((y + SIDE - e) % SIDE) * 2
        for src, k in ((rows[e], near + core_at), (rows[SIDE + e], near + 1 - core_at)):
            copies.append((src.at[0], ru_ref.at[k]))
            copies.append((src.at[1], rv_ref.at[k]))
    copies.append((band_ref, out_ref))
    row_copies = run_copies(copies, sems)
    base = len(copies)

    @pl.when(core_at == 0)
    def _():
        for copy in run_copies(slab_copies(meta, even[:4], even[4:], u_ref, v_ref, None, None), sems, base):
            copy.wait()

    @pl.when(core_at != 0)
    def _():
        for copy in run_copies(slab_copies(meta, odd[:4], odd[4:], u_ref, v_ref, None, None), sems, base):
            copy.wait()

    for copy in row_copies:
        copy.wait()
    dout_ref[...] = diag_ref[...]

    def panel(k, _):
        rank = meta[4 + k]
        uk = u_ref[k]
        vk = masked(v_ref[k].astype(jnp.float32), rank).astype(jnp.bfloat16)
        core = tn(rv_ref[k], vk).astype(jnp.bfloat16)
        left = jnp.dot(ru_ref[k], core, preferred_element_type=jnp.float32).astype(jnp.bfloat16)
        for s in range(0, n, 256):
            out_ref[s:s + 256, :] = out_ref[s:s + 256, :] - nt(left[s:s + 256], uk)

        @pl.when(column != 0)
        def _():
            own = tn(vk, vk).astype(jnp.bfloat16)
            part = jnp.dot(u_ref[k, at, :], own, preferred_element_type=jnp.float32).astype(jnp.bfloat16)
            dout_ref[...] = dout_ref[...] - nt(part, uk)
        return 0
    lax.fori_loop(0, panels, panel, 0)

    @pl.when(column == 0)
    def _():
        last = run_copies([(l_hbm, l_ref), (inv_hbm, inv_ref)], sems, base)
        for copy in last:
            copy.wait()
        dout_ref[...] = l_ref[at, :]
        solve_body(out_ref, l_ref, inv_ref, out_ref, xh_ref, xl_ref)


def moved(value, pairs):
    return lax.ppermute(value, AXES, pairs)


def along(axis, step, parity):
    pairs = []
    for x in range(SIDE):
        for z in range(SIDE):
            for col in range(parity, 8, 2):
                to = ((x + step) % SIDE, z) if axis == "x" else (x, (z + step) % SIDE)
                pairs.append(((x * SIDE + z) * 8 + col, (to[0] * SIDE + to[1]) * 8 + col))
    return pairs


def across(change):
    return [(row * 8 + col, row * 8 + change(col)) for row in range(16) for col in range(8)]


def spread(first, second, parity, after=None):
    a = [first] + [moved(first, along("x", d, parity)) for d in (1, 2, 3)]
    b = [second] + [moved(second, along("z", d, parity)) for d in (1, 2, 3)]
    a, b = lax.optimization_barrier((a, b))
    if after is not None:
        a, b, held = lax.optimization_barrier((a, b, after()))
    a, b = jnp.stack(a), jnp.stack(b)
    fs = [a] + [moved(a, along("z", d, parity)) for d in (1, 2, 3)]
    gs = [b] + [moved(b, along("x", d, parity)) for d in (1, 2, 3)]
    if after is not None:
        return fs, gs, held
    return lax.optimization_barrier((fs, gs))


def shards(band, diag, row_factors, row_ranks, col_factors, col_ranks):
    column = lax.axis_index("cols")
    slab = lax.axis_index("rows")
    panels, slab_rows = col_factors.shape[0], diag.shape[1]
    order, rank = row_factors.shape[3], row_factors.shape[4]
    own_ranks = lax.dynamic_index_in_dim(col_ranks, column, 0, keepdims=False)
    meta = jnp.concatenate([jnp.stack([column, slab // SIDE, slab % SIDE, slab]).astype(jnp.int32), own_ranks])

    mine = row_factors[0, 0]
    kept = (jnp.arange(rank, dtype=jnp.int32) < row_ranks[0, 0])[None, None, :] | (jnp.arange(2) == 0)[:, None, None]
    mine = jnp.where(kept, mine, jnp.zeros((), mine.dtype))

    own = lax.all_to_all(col_factors, "cols", split_axis=0, concat_axis=1, tiled=True)[0]
    pieces = diag[0].reshape(slab_rows, 4, rank).transpose(1, 0, 2)
    rounded = lax.reduce_precision(pieces, exponent_bits=8, mantissa_bits=7)
    high = rounded.astype(jnp.bfloat16)
    low = (pieces - rounded).astype(jnp.bfloat16)
    own, mine = lax.optimization_barrier((own, mine))
    near = [mine] + [moved(mine, across(lambda c, d=d: ((c // 2 + d) % SIDE) * 2 + c % 2)) for d in (1, 2, 3)]
    sides, bases = own[:, 1], own[:, 0]
    fs, gs = spread(jnp.concatenate([sides, high]), jnp.concatenate([bases, low]), 0)

    token = moved(jnp.stack([p[0, 0, :8, :128] for p in fs[1:] + gs[1:]]), across(lambda c: c ^ 1))
    held = jnp.where(jnp.any(token != token), jnp.ones((), sides.dtype), jnp.zeros((), sides.dtype))
    sides, bases = lax.optimization_barrier((sides + held, bases + held))
    hbm = pl.BlockSpec(memory_space=pl.ANY)
    smem = pl.BlockSpec(memory_space=pltpu.SMEM)
    vmem = pl.BlockSpec(memory_space=pltpu.VMEM)
    stack = pltpu.VMEM((panels, order, rank), jnp.bfloat16)
    quarter = pltpu.VMEM((4, order, rank), jnp.bfloat16)
    square = jax.ShapeDtypeStruct((order, order), jnp.float32)
    params = pltpu.CompilerParams(vmem_limit_bytes=60 << 20)
    call = pl.pallas_call(
        factor_kernel,
        out_shape=(square, jax.ShapeDtypeStruct((order, NB), jnp.float32)),
        in_specs=[smem] + [hbm] * 8,
        out_specs=(vmem, vmem),
        scratch_shapes=[stack, stack, quarter, quarter, pltpu.VMEM((order, order), jnp.float32),
                        pltpu.VMEM((NB, 2 * NB), jnp.float32), pltpu.SemaphoreType.DMA((64,))],
        cost_estimate=pl.CostEstimate(flops=60_000_000_000, bytes_accessed=20_000_000, transcendentals=0),
        compiler_params=params, name="factor")
    far = [moved(p, across(lambda c: c ^ 1)) for p in near]
    odd_fs, odd_gs, (factor, inverses) = spread(sides, bases, 1, lambda: call(meta, *fs, *gs))
    tile, slab_out = pl.pallas_call(
        tile_kernel,
        out_shape=(square, jax.ShapeDtypeStruct((slab_rows, order), jnp.float32)),
        in_specs=[smem] + [hbm] * 25 + [vmem, hbm, hbm],
        out_specs=(vmem, vmem),
        scratch_shapes=[stack] * 4 + [pltpu.VMEM((order, order), jnp.float32), pltpu.VMEM((order, NB), jnp.float32),
                        pltpu.VMEM((order, order), jnp.bfloat16), pltpu.VMEM((order, order), jnp.bfloat16),
                        pltpu.SemaphoreType.DMA((64,))],
        cost_estimate=pl.CostEstimate(flops=10_000_000_000, bytes_accessed=40_000_000, transcendentals=0),
        compiler_params=params, name="tile")(
            meta, *fs, *gs, *odd_fs, *odd_gs, *near, *far, band[0, 0], diag[0], factor, inverses)
    return tile[None, None], slab_out[None]


def solution(mesh):
    placed = (
        P("rows", "cols", None, None),
        P("cols", "rows", None),
        P("rows", "cols", None, None, None),
        P("rows", "cols"),
        P(None, "cols", None, "rows", None),
        P(),
    )
    return jax.shard_map(
        shards,
        mesh=mesh,
        in_specs=placed,
        out_specs=(P("rows", "cols", None, None), P("cols", "rows", None)),
        check_vma=False,
    )
```

```python
import jax
import jax.numpy as jnp
from jax import lax
from jax.experimental import pallas as pl
from jax.experimental.pallas import tpu as pltpu
from jax.sharding import PartitionSpec as P

NB = 128
G = 8
SIDE = 4
AXES = ("rows", "cols")


def split2(x):
    hi = x.astype(jnp.bfloat16)
    lo = (x - hi.astype(jnp.float32)).astype(jnp.bfloat16)
    return hi, lo

def nt(a, b):
    return lax.dot_general(a, b, (((1,), (1,)), ((), ())), preferred_element_type=jnp.float32)

def nt3(ah, al, bh, bl):
    return nt(jnp.concatenate([ah, al, ah], axis=1), jnp.concatenate([bh, bh, bl], axis=1))

def factor_block(t_ref):
    for g in range(NB // G):
        v = t_ref[g * G:(g + 1) * G, :]
        cols = [jnp.broadcast_to(v[:, g * G + j:g * G + j + 1], (G, NB)) for j in range(G)]
        b = [[jnp.broadcast_to(cols[j][s:s + 1, :], (G, NB)) if s >= j else None for j in range(G)] for s in range(G)]
        low = [[None] * G for _ in range(G)]
        rinv = [None] * G
        r = [jnp.broadcast_to(v[s:s + 1, :], (G, 2 * NB)) for s in range(G)]
        two = lambda x: jnp.concatenate([x, x], axis=1)
        for j in range(G):
            rinv[j] = lax.rsqrt(b[j][j])
            for s in range(j + 1, G):
                low[s][j] = b[s][j] * rinv[j]
            for t in range(j + 1, G):
                for s in range(t, G):
                    b[s][t] = b[s][t] - low[s][j] * low[t][j]
            r[j] = r[j] * two(rinv[j])
            for s in range(j + 1, G):
                r[s] = r[s] - two(low[s][j]) * r[j]
        m = [None] * G
        for s in reversed(range(G)):
            acc = r[s]
            for t in range(s + 1, G):
                acc = acc - two(low[t][s]) * m[t]
            m[s] = acc * two(rinv[s])
        sub = lax.broadcasted_iota(jnp.int32, (G, 2 * NB), 0)
        out = r[0]
        for s in range(1, G):
            out = jnp.where(sub == s, r[s], out)
        t_ref[g * G:(g + 1) * G, :] = out
        for rb in range(g + 1, NB // G):
            w = t_ref[rb * G:(rb + 1) * G, :]
            acc = w
            for j in range(G):
                wc = jnp.broadcast_to(w[:, g * G + j:g * G + j + 1], (G, NB))
                acc = acc - two(wc) * m[j]
            t_ref[rb * G:(rb + 1) * G, :] = acc

def chol_body(a_ref, inv_ref, t_ref, beside):
    n = a_ref.shape[0]
    nblk = n // NB
    ri = lax.broadcasted_iota(jnp.int32, (NB, NB), 0)
    ci = lax.broadcasted_iota(jnp.int32, (NB, NB), 1)

    def step(j, _):
        o = pl.multiple_of(j * NB, NB)
        t_ref[:, :NB] = a_ref[pl.ds(o, NB), pl.ds(o, NB)]
        t_ref[:, NB:] = jnp.where(ri == ci, 1.0, 0.0)
        factor_block(t_ref)
        beside(j)
        inv = t_ref[:, NB:]
        inv_ref[pl.ds(o, NB), :] = inv
        low = jnp.where(ri >= ci, t_ref[:, :NB].T, 0.0)
        ih, il = split2(inv)
        for v in range(nblk // 2):
            lo_row = 2 * NB * v
            @pl.when((j + 1) // 2 == v)
            def _():
                p = a_ref[lo_row:, pl.ds(o, NB)]
                ph, plo = split2(p)
                x = nt3(ph, plo, ih, il)
                rows = lax.broadcasted_iota(jnp.int32, x.shape, 0) + lo_row
                x = jnp.where(rows >= o + NB, x, 0.0)
                a_ref[lo_row:, pl.ds(o, NB)] = x
                xh, xl = split2(x)
                c = nt3(xh, xl, xh, xl)
                a_ref[lo_row:, lo_row:] = a_ref[lo_row:, lo_row:] - c
        a_ref[pl.ds(o, NB), pl.ds(o, NB)] = low
        return 0
    lax.fori_loop(0, nblk, step, 0)

def solve_body(b_ref, l_ref, inv_ref, x_ref, xh_ref, xl_ref, done):
    n = b_ref.shape[0]
    for j in range(n // NB):
        s = slice(j * NB, (j + 1) * NB)
        ih, il = split2(inv_ref[s, :])
        acc = b_ref[:, s]
        if j:
            lh, ll = split2(l_ref[s, :j * NB])
            acc = acc - nt(xh_ref[:, :j * NB], lh) - nt(xl_ref[:, :j * NB], lh) - nt(xh_ref[:, :j * NB], ll)
        ah, al = split2(acc)
        x = nt3(ah, al, ih, il)
        x_ref[:, s] = x
        done(j, s)
        xh, xl = split2(x)
        xh_ref[:, s] = xh
        xl_ref[:, s] = xl


def tn(a, b):
    return lax.dot_general(a, b, (((0,), (0,)), ((), ())), preferred_element_type=jnp.float32)


def masked(core, rank_a, rank_b):
    kept = lax.broadcasted_iota(jnp.int32, core.shape, 1) < rank_b
    if rank_a is not None:
        kept = kept & (lax.broadcasted_iota(jnp.int32, core.shape, 0) < rank_a)
    return jnp.where(kept, core, 0.0).astype(jnp.bfloat16)


def started(pairs, sems, first=0):
    copies = [pltpu.make_async_copy(src, dst, sems.at[first + n]) for n, (src, dst) in enumerate(pairs)]
    for copy in copies:
        copy.start()
    return copies


def waited(copies):
    for copy in copies:
        copy.wait()


def slab_copies(meta, fs, gs, u_ref, v_ref, first, count):
    x, z = meta[1], meta[2]
    pairs = []
    for e in range(SIDE):
        for d in range(SIDE):
            slab = ((x + SIDE - d) % SIDE) * SIDE + (z + SIDE - e) % SIDE
            at = pl.ds(pl.multiple_of(slab * 64, 64), 64)
            to = pl.ds(0, count) if first >= 8 else pl.ds(first, count)
            pairs.append((fs[e].at[d, pl.ds(first, count)], v_ref.at[to, at, :]))
            pairs.append((gs[d].at[e, pl.ds(first, count)], u_ref.at[to, at, :]))
    return pairs


def row_copies(meta, rows, ru_ref, rv_ref):
    y, core_at = meta[0] // 2, meta[0] % 2
    pairs = []
    for e in range(SIDE):
        near = ((y + SIDE - e) % SIDE) * 2
        for src, k in ((rows[e], near + core_at), (rows[SIDE + e], near + 1 - core_at)):
            pairs.append((src.at[0], ru_ref.at[k]))
            pairs.append((src.at[1], rv_ref.at[k]))
    return pairs


def tile_panel(meta, k, tile_ref, u_ref, v_ref, ru_ref, rv_ref):
    n = tile_ref.shape[0]
    core = jnp.dot(rv_ref[k, 0:256], v_ref[k, 0:256], preferred_element_type=jnp.float32)
    for q in range(256, n, 256):
        core = core + jnp.dot(rv_ref[k, q:q + 256], v_ref[k, q:q + 256], preferred_element_type=jnp.float32)
    core = masked(core, None, meta[4 + k])
    uk = u_ref[k]
    for s in range(0, n, 256):
        left = jnp.dot(ru_ref[k, s:s + 256], core, preferred_element_type=jnp.float32).astype(jnp.bfloat16)
        tile_ref[s:s + 256, :] = tile_ref[s:s + 256, :] - nt(left, uk)


def column_kernel(meta, *refs):
    fs, gs, rows = refs[0:4], refs[4:8], refs[8:16]
    band_hbm, out_hbm, dout_hbm = refs[16:19]
    (u_ref, v_ref, hi_ref, lo_ref, ru_ref, rv_ref, tile_ref, acc_ref, l_ref, inv_ref, t_ref, xh_ref, xl_ref, sems) = refs[19:]
    n = l_ref.shape[0]

    @pl.when(meta[0] == 0)
    def _():
        one = started(slab_copies(meta, fs, gs, u_ref, v_ref, 0, 4), sems, 0)
        two = started(slab_copies(meta, fs, gs, u_ref, v_ref, 4, 4), sems, 32)
        three = started(slab_copies(meta, fs, gs, lo_ref, hi_ref, 8, 4), sems, 64)
        four = started(row_copies(meta, rows, ru_ref, rv_ref) + [(band_hbm, tile_ref)], sems, 96)
        acc_ref[...] = jnp.zeros_like(acc_ref)

        def panel(k, _):
            rank = meta[4 + k]
            vk, uk = v_ref[k], u_ref[k]
            core = masked(tn(vk, vk), rank, rank)
            for s in range(0, n, 256):
                left = jnp.dot(u_ref[k, s:s + 256], core, preferred_element_type=jnp.float32).astype(jnp.bfloat16)
                acc_ref[s:s + 256, :] = acc_ref[s:s + 256, :] - nt(left, uk)
            return 0
        waited(one)
        lax.fori_loop(0, 4, panel, 0)
        waited(two)
        lax.fori_loop(4, 8, panel, 0)
        waited(three)
        for q in range(4):
            s = slice(q * 256, (q + 1) * 256)
            acc_ref[:, s] = acc_ref[:, s] + (hi_ref[q].astype(jnp.float32) + lo_ref[q].astype(jnp.float32))
        for i in range(n // NB):
            si = slice(i * NB, (i + 1) * NB)
            for j in range(i + 1):
                sj = slice(j * NB, (j + 1) * NB)
                l_ref[si, sj] = (acc_ref[si, sj] + acc_ref[sj, si].T) * 0.5
        waited(four)
        chol_body(l_ref, inv_ref, t_ref, lambda j: tile_panel(meta, j, tile_ref, u_ref, v_ref, ru_ref, rv_ref))
        for j in range(n // NB - 1):
            l_ref[j * NB:(j + 1) * NB, (j + 1) * NB:] = jnp.zeros((NB, n - (j + 1) * NB), jnp.float32)
        last = started([(l_ref.at[pl.ds(pl.multiple_of(meta[3] * 64, 64), 64), :], dout_hbm)], sems, 0)

        def done(j, s):
            last.extend(started([(tile_ref.at[:, s], out_hbm.at[:, s])], sems, 1 + j))
        solve_body(tile_ref, l_ref, inv_ref, tile_ref, xh_ref, xl_ref, done)
        waited(last)


def tile_kernel(meta, *refs):
    even, odd, rows = refs[0:8], refs[8:16], refs[16:24]
    band_hbm, diag_hbm, _, _, out_hbm, dout_hbm = refs[24:30]
    u_ref, v_ref, ru_ref, rv_ref, tile_ref, slab_ref, sems = refs[30:]
    panels = u_ref.shape[0]
    at = pl.ds(pl.multiple_of(meta[3] * 64, 64), 64)

    @pl.when(meta[0] != 0)
    def _():
        four = started(row_copies(meta, rows, ru_ref, rv_ref) + [(band_hbm, tile_ref), (diag_hbm, slab_ref)], sems, 64)

        @pl.when(meta[0] % 2 == 0)
        def _():
            waited(started(slab_copies(meta, even[:4], even[4:], u_ref, v_ref, 0, 4)
                           + slab_copies(meta, even[:4], even[4:], u_ref, v_ref, 4, 4), sems, 0))

        @pl.when(meta[0] % 2 != 0)
        def _():
            waited(started(slab_copies(meta, odd[:4], odd[4:], u_ref, v_ref, 0, 4)
                           + slab_copies(meta, odd[:4], odd[4:], u_ref, v_ref, 4, 4), sems, 0))
        waited(four)

        def panel(k, _):
            tile_panel(meta, k, tile_ref, u_ref, v_ref, ru_ref, rv_ref)
            rank = meta[4 + k]
            vk = v_ref[k]
            core = masked(tn(vk, vk), rank, rank)
            part = jnp.dot(u_ref[k, at, :], core, preferred_element_type=jnp.float32).astype(jnp.bfloat16)
            slab_ref[...] = slab_ref[...] - nt(part, u_ref[k])
            return 0
        lax.fori_loop(0, panels, panel, 0)
        waited(started([(tile_ref, out_hbm), (slab_ref, dout_hbm)], sems, 0))


def moved(value, pairs):
    return lax.ppermute(value, AXES, pairs)


def along(axis, step, parity):
    pairs = []
    for x in range(SIDE):
        for z in range(SIDE):
            for col in range(parity, 8, 2):
                to = ((x + step) % SIDE, z) if axis == "x" else (x, (z + step) % SIDE)
                pairs.append(((x * SIDE + z) * 8 + col, (to[0] * SIDE + to[1]) * 8 + col))
    return pairs


def across(change):
    return [(row * 8 + col, row * 8 + change(col)) for row in range(16) for col in range(8)]


def first_leg(first, second, parity):
    a = [first] + [moved(first, along("x", d, parity)) for d in (1, 3, 2)]
    b = [second] + [moved(second, along("z", d, parity)) for d in (1, 3, 2)]
    return a, b


def second_leg(a, b, parity):
    a, b = jnp.stack([a[0], a[1], a[3], a[2]]), jnp.stack([b[0], b[1], b[3], b[2]])
    fs = [a] + [moved(a, along("z", d, parity)) for d in (1, 2, 3)]
    gs = [b] + [moved(b, along("x", d, parity)) for d in (1, 2, 3)]
    return fs, gs


def shards(band, diag, row_factors, row_ranks, col_factors, col_ranks):
    column = lax.axis_index("cols")
    slab = lax.axis_index("rows")
    panels, slab_rows = col_factors.shape[0], diag.shape[1]
    order, rank = row_factors.shape[3], row_factors.shape[4]
    own_ranks = lax.dynamic_index_in_dim(col_ranks, column, 0, keepdims=False)
    meta = jnp.concatenate([jnp.stack([column, slab // SIDE, slab % SIDE, slab]).astype(jnp.int32), own_ranks])

    turned = row_factors[0, 0, 1].reshape(order // rank, rank, rank).transpose(0, 2, 1)
    kept = (jnp.arange(rank, dtype=jnp.int32) < row_ranks[0, 0])[None, :, None]
    turned = jnp.where(kept, turned, jnp.zeros((), turned.dtype)).reshape(order, rank)
    mine = jnp.stack([row_factors[0, 0, 0], turned])

    own = lax.all_to_all(col_factors, "cols", split_axis=0, concat_axis=1, tiled=True)[0]
    pieces = diag[0].reshape(slab_rows, 4, rank).transpose(1, 0, 2)
    rounded = lax.reduce_precision(pieces, exponent_bits=8, mantissa_bits=7)
    high = rounded.astype(jnp.bfloat16)
    low = (pieces - rounded).astype(jnp.bfloat16)
    own, mine, meta, high, low = lax.optimization_barrier((own, mine, meta, high, low))
    near = [mine] + [moved(mine, across(lambda c, d=d: ((c // 2 + d) % SIDE) * 2 + c % 2)) for d in (1, 2, 3)]
    sides, bases = own[:, 1], own[:, 0]
    a, b = lax.optimization_barrier(first_leg(jnp.concatenate([sides, high]), jnp.concatenate([bases, low]), 0))
    fs, gs = second_leg(a, b, 0)
    odd_legs = first_leg(sides, bases, 1)
    far = [moved(p, across(lambda c: c ^ 1)) for p in near]
    fs, gs, near, far = lax.optimization_barrier((fs, gs, near, far))
    token = moved(fs[1][0, 0, :8, :128], across(lambda c: c ^ 1))

    hbm = pl.BlockSpec(memory_space=pl.ANY)
    smem = pl.BlockSpec(memory_space=pltpu.SMEM)
    stack = pltpu.VMEM((panels, order, rank), jnp.bfloat16)
    quarter = pltpu.VMEM((4, order, rank), jnp.bfloat16)
    square = pltpu.VMEM((order, order), jnp.float32)
    outs = (jax.ShapeDtypeStruct((order, order), jnp.float32), jax.ShapeDtypeStruct((slab_rows, order), jnp.float32))
    params = pltpu.CompilerParams(vmem_limit_bytes=60 << 20)
    tile, slab_out = pl.pallas_call(
        column_kernel,
        out_shape=outs,
        in_specs=[smem] + [hbm] * 17,
        out_specs=(hbm, hbm),
        scratch_shapes=[stack, stack, quarter, quarter, stack, stack, square, square, square,
                        pltpu.VMEM((order, NB), jnp.float32), pltpu.VMEM((NB, 2 * NB), jnp.float32),
                        pltpu.VMEM((order, order), jnp.bfloat16), pltpu.VMEM((order, order), jnp.bfloat16),
                        pltpu.SemaphoreType.DMA((128,))],
        cost_estimate=pl.CostEstimate(flops=60_000_000_000, bytes_accessed=20_000_000, transcendentals=0),
        compiler_params=params, name="column")(meta, *fs, *gs, *near, *far, band[0, 0])

    token, odd_legs, tile, slab_out = lax.optimization_barrier((token, odd_legs, tile, slab_out))
    held = jnp.where(token[0, 0] != token[0, 0], jnp.ones((), token.dtype), jnp.zeros((), token.dtype))
    odd_a, odd_b = odd_legs
    odd_fs, odd_gs = second_leg([p + held for p in odd_a], [p + held for p in odd_b], 1)
    tile, slab_out = pl.pallas_call(
        tile_kernel,
        out_shape=outs,
        in_specs=[smem] + [hbm] * 28,
        out_specs=(hbm, hbm),
        scratch_shapes=[stack] * 4 + [square, pltpu.VMEM((slab_rows, order), jnp.float32), pltpu.SemaphoreType.DMA((96,))],
        input_output_aliases={27: 0, 28: 1},
        cost_estimate=pl.CostEstimate(flops=10_000_000_000, bytes_accessed=40_000_000, transcendentals=0),
        compiler_params=params, name="tile")(
            meta, *fs, *gs, *odd_fs, *odd_gs, *near, *far, band[0, 0], diag[0], tile, slab_out)
    return tile[None, None], slab_out[None]


def solution(mesh):
    placed = (
        P("rows", "cols", None, None),
        P("cols", "rows", None),
        P("rows", "cols", None, None, None),
        P("rows", "cols"),
        P(None, "cols", None, "rows", None),
        P(),
    )
    return jax.shard_map(
        shards,
        mesh=mesh,
        in_specs=placed,
        out_specs=(P("rows", "cols", None, None), P("cols", "rows", None)),
        check_vma=False,
    )
```

```python
import jax
import jax.numpy as jnp
from jax import lax
from jax.experimental import pallas as pl
from jax.experimental.pallas import tpu as pltpu
from jax.sharding import PartitionSpec as P

NB = 128
G = 8
SIDE = 4
AXES = ("rows", "cols")


def split2(x):
    hi = x.astype(jnp.bfloat16)
    lo = (x - hi.astype(jnp.float32)).astype(jnp.bfloat16)
    return hi, lo

def nt(a, b):
    return lax.dot_general(a, b, (((1,), (1,)), ((), ())), preferred_element_type=jnp.float32)

def nt3(ah, al, bh, bl):
    return nt(jnp.concatenate([ah, al, ah], axis=1), jnp.concatenate([bh, bh, bl], axis=1))

def lane_splat(x, lane, one):
    return jnp.broadcast_to(x[:, lane:lane + 1], x.shape) * one


def row_splat(x, s):
    return jnp.broadcast_to(x[s:s + 1, :], x.shape)


def factor_block(t_ref, up_ref, one_ref):
    one = one_ref[...]
    sub = lax.broadcasted_iota(jnp.int32, (G, NB), 0)
    lane = lax.broadcasted_iota(jnp.int32, (G, NB), 1)
    count = NB // G
    first = t_ref[0:G, :]
    diag = [lane_splat(first, c, one) for c in range(G)]
    for g in range(count):
        base = g * G
        v = t_ref[base:base + G, :]
        b = [[row_splat(diag[j], s) if s >= j else None for j in range(G)] for s in range(G)]
        more = g + 1 < count
        if more:
            below = t_ref[base + G:base + 2 * G, :]
            wn = [lane_splat(below, base + j, one) for j in range(G)]
            diag = [lane_splat(below, base + G + c, one) for c in range(G)]
        inside = (lane >= base) & (lane < base + G)
        vi = jnp.where(inside, jnp.where(lane - base == sub, 1.0, 0.0), v)
        low = [[None] * G for _ in range(G)]
        rinv = [None] * G
        ra = [row_splat(v, s) for s in range(G)]
        r = [row_splat(vi, s) for s in range(G)]
        for j in range(G):
            rinv[j] = lax.rsqrt(b[j][j])
            for s in range(j + 1, G):
                low[s][j] = b[s][j] * rinv[j]
            for t in range(j + 1, G):
                for s in range(t, G):
                    b[s][t] = b[s][t] - low[s][j] * low[t][j]
            if more:
                ln = wn[j] * rinv[j]
                for t in range(j + 1, G):
                    wn[t] = wn[t] - ln * low[t][j]
                for c in range(G):
                    diag[c] = diag[c] - ln * row_splat(ln, c)
            ra[j] = ra[j] * rinv[j]
            r[j] = r[j] * rinv[j]
            for s in range(j + 1, G):
                ra[s] = ra[s] - low[s][j] * ra[j]
                r[s] = r[s] - low[s][j] * r[j]
        out, outa = r[0], ra[0]
        for s in range(1, G):
            out = jnp.where(sub == s, r[s], out)
            outa = jnp.where(sub == s, ra[s], outa)
        up_ref[base:base + G, :] = outa
        t_ref[base:base + G, :] = out
        if more:
            m = [None] * G
            for s in reversed(range(G)):
                acc = r[s]
                for t in range(s + 1, G):
                    acc = acc - low[t][s] * m[t]
                m[s] = acc * rinv[s]
            for rb in range(g + 1, count):
                w = t_ref[rb * G:(rb + 1) * G, :]
                acc = jnp.where(inside, 0.0, w)
                for j in range(G):
                    acc = acc - lane_splat(w, base + j, one) * m[j]
                t_ref[rb * G:(rb + 1) * G, :] = acc


def chol_body(a_ref, inv_ref, t_ref, up_ref, one_ref, beside):
    n = a_ref.shape[0]
    nblk = n // NB
    ri = lax.broadcasted_iota(jnp.int32, (NB, NB), 0)
    ci = lax.broadcasted_iota(jnp.int32, (NB, NB), 1)

    def step(j, _):
        o = pl.multiple_of(j * NB, NB)
        t_ref[...] = a_ref[pl.ds(o, NB), pl.ds(o, NB)]
        factor_block(t_ref, up_ref, one_ref)
        beside(j)
        inv = jnp.where(ri >= ci, t_ref[...], 0.0)
        inv_ref[pl.ds(o, NB), :] = inv
        low = jnp.where(ri >= ci, up_ref[...].T, 0.0)
        ih, il = split2(inv)
        for v in range(nblk // 2):
            lo_row = 2 * NB * v
            @pl.when((j + 1) // 2 == v)
            def _():
                p = a_ref[lo_row:, pl.ds(o, NB)]
                ph, plo = split2(p)
                x = nt3(ph, plo, ih, il)
                rows = lax.broadcasted_iota(jnp.int32, x.shape, 0) + lo_row
                x = jnp.where(rows >= o + NB, x, 0.0)
                a_ref[lo_row:, pl.ds(o, NB)] = x
                xh, xl = split2(x)
                c = nt3(xh, xl, xh, xl)
                a_ref[lo_row:, lo_row:] = a_ref[lo_row:, lo_row:] - c
        a_ref[pl.ds(o, NB), pl.ds(o, NB)] = low
        return 0
    lax.fori_loop(0, nblk, step, 0)

def solve_body(b_ref, l_ref, inv_ref, x_ref, xh_ref, xl_ref, done):
    n = b_ref.shape[0]
    for j in range(n // NB):
        s = slice(j * NB, (j + 1) * NB)
        ih, il = split2(inv_ref[s, :])
        acc = b_ref[:, s]
        if j:
            lh, ll = split2(l_ref[s, :j * NB])
            acc = acc - nt(xh_ref[:, :j * NB], lh) - nt(xl_ref[:, :j * NB], lh) - nt(xh_ref[:, :j * NB], ll)
        ah, al = split2(acc)
        x = nt3(ah, al, ih, il)
        x_ref[:, s] = x
        done(j, s)
        xh, xl = split2(x)
        xh_ref[:, s] = xh
        xl_ref[:, s] = xl


def tn(a, b):
    return lax.dot_general(a, b, (((0,), (0,)), ((), ())), preferred_element_type=jnp.float32)


def masked(core, rank_a, rank_b):
    kept = lax.broadcasted_iota(jnp.int32, core.shape, 1) < rank_b
    if rank_a is not None:
        kept = kept & (lax.broadcasted_iota(jnp.int32, core.shape, 0) < rank_a)
    return jnp.where(kept, core, 0.0).astype(jnp.bfloat16)


def started(pairs, sems, first=0):
    copies = [pltpu.make_async_copy(src, dst, sems.at[first + n]) for n, (src, dst) in enumerate(pairs)]
    for copy in copies:
        copy.start()
    return copies


def waited(copies):
    for copy in copies:
        copy.wait()


def slab_copies(meta, fs, gs, u_ref, v_ref, first, count, to=None):
    x, z = meta[1], meta[2]
    pairs = []
    for e in range(SIDE):
        for d in range(SIDE):
            slab = ((x + SIDE - d) % SIDE) * SIDE + (z + SIDE - e) % SIDE
            at = pl.ds(pl.multiple_of(slab * 64, 64), 64)
            pairs.append((fs[e].at[d, pl.ds(first, count)], v_ref.at[pl.ds(first if to is None else to, count), at, :]))
            pairs.append((gs[d].at[e, pl.ds(first, count)], u_ref.at[pl.ds(first if to is None else to, count), at, :]))
    return pairs


def row_copies(meta, rows, ru_ref, rv_ref):
    y, core_at = meta[0] // 2, meta[0] % 2
    pairs = []
    for e in range(SIDE):
        near = ((y + SIDE - e) % SIDE) * 2
        for src, k in ((rows[e], near + core_at), (rows[SIDE + e], near + 1 - core_at)):
            pairs.append((src.at[0], ru_ref.at[k]))
            pairs.append((src.at[1], rv_ref.at[k]))
    return pairs


def tile_panel(meta, k, tile_ref, u_ref, v_ref, ru_ref, rv_ref):
    n = tile_ref.shape[0]
    core = jnp.dot(rv_ref[k, 0:256], v_ref[k, 0:256], preferred_element_type=jnp.float32)
    for q in range(256, n, 256):
        core = core + jnp.dot(rv_ref[k, q:q + 256], v_ref[k, q:q + 256], preferred_element_type=jnp.float32)
    core = masked(core, None, meta[4 + k])
    uk = u_ref[k]
    for s in range(0, n, 256):
        left = jnp.dot(ru_ref[k, s:s + 256], core, preferred_element_type=jnp.float32).astype(jnp.bfloat16)
        tile_ref[s:s + 256, :] = tile_ref[s:s + 256, :] - nt(left, uk)


def column_kernel(meta, *refs):
    fs, gs, rows = refs[0:4], refs[4:8], refs[8:16]
    band_hbm, out_hbm, dout_hbm = refs[16:19]
    (u_ref, v_ref, hi_ref, lo_ref, ru_ref, rv_ref, tile_ref, acc_ref, l_ref, inv_ref, t_ref, up_ref, one_ref, xh_ref, xl_ref, sems) = refs[19:]
    n = l_ref.shape[0]

    @pl.when(meta[0] == 0)
    def _():
        one = started(slab_copies(meta, fs, gs, u_ref, v_ref, 0, 4), sems, 0)
        two = started(slab_copies(meta, fs, gs, u_ref, v_ref, 4, 4), sems, 32)
        three = started(slab_copies(meta, fs, gs, lo_ref, hi_ref, 8, 4, 0), sems, 64)
        acc_ref[...] = jnp.zeros_like(acc_ref)

        four = [pltpu.make_async_copy(src, dst, sems.at[96 + n])
                for n, (src, dst) in enumerate(row_copies(meta, rows, ru_ref, rv_ref) + [(band_hbm, tile_ref)])]

        def panel(k, _):
            @pl.when(k == 4)
            def _():
                waited(two)
                for copy in four:
                    copy.start()
            rank = meta[4 + k]
            vk, uk = v_ref[k], u_ref[k]
            core = masked(tn(vk, vk), rank, rank)
            for s in range(0, n, 256):
                left = jnp.dot(u_ref[k, s:s + 256], core, preferred_element_type=jnp.float32).astype(jnp.bfloat16)
                acc_ref[s:s + 256, :] = acc_ref[s:s + 256, :] - nt(left, uk)
            return 0
        waited(one)
        lax.fori_loop(0, 8, panel, 0)
        waited(three)
        for q in range(4):
            s = slice(q * 256, (q + 1) * 256)
            acc_ref[:, s] = acc_ref[:, s] + (hi_ref[q].astype(jnp.float32) + lo_ref[q].astype(jnp.float32))
        for i in range(n // NB):
            si = slice(i * NB, (i + 1) * NB)
            for j in range(i + 1):
                sj = slice(j * NB, (j + 1) * NB)
                l_ref[si, sj] = (acc_ref[si, sj] + acc_ref[sj, si].T) * 0.5
        waited(four)
        one_ref[...] = jnp.ones_like(one_ref)
        chol_body(l_ref, inv_ref, t_ref, up_ref, one_ref, lambda j: tile_panel(meta, j, tile_ref, u_ref, v_ref, ru_ref, rv_ref))
        for j in range(n // NB - 1):
            l_ref[j * NB:(j + 1) * NB, (j + 1) * NB:] = jnp.zeros((NB, n - (j + 1) * NB), jnp.float32)
        last = started([(l_ref.at[pl.ds(pl.multiple_of(meta[3] * 64, 64), 64), :], dout_hbm)], sems, 0)

        def done(j, s):
            last.extend(started([(tile_ref.at[:, s], out_hbm.at[:, s])], sems, 1 + j))
        solve_body(tile_ref, l_ref, inv_ref, tile_ref, xh_ref, xl_ref, done)
        waited(last)


def column_scratch(panels, order, rank):
    stack = pltpu.VMEM((panels, order, rank), jnp.bfloat16)
    quarter = pltpu.VMEM((4, order, rank), jnp.bfloat16)
    square = pltpu.VMEM((order, order), jnp.float32)
    block = pltpu.VMEM((NB, NB), jnp.float32)
    return [stack, stack, quarter, quarter, stack, stack, square, square, square,
            pltpu.VMEM((order, NB), jnp.float32), block, block, pltpu.VMEM((G, NB), jnp.float32),
            pltpu.VMEM((order, order), jnp.bfloat16), pltpu.VMEM((order, order), jnp.bfloat16),
            pltpu.SemaphoreType.DMA((128,))]


def tile_kernel(meta, *refs):
    even, odd, rows = refs[0:8], refs[8:16], refs[16:24]
    band_hbm, diag_hbm, _, _, out_hbm, dout_hbm = refs[24:30]
    u_ref, v_ref, ru_ref, rv_ref, tile_ref, slab_ref, sems, row_sems = refs[30:]
    panels, n = u_ref.shape[0], tile_ref.shape[0]
    at = pl.ds(pl.multiple_of(meta[3] * 64, 64), 64)
    y, core_at = meta[0] // 2, meta[0] % 2

    @pl.when(meta[0] != 0)
    def _():
        four = started([(band_hbm, tile_ref), (diag_hbm, slab_ref)], sems, 128)

        def start_columns(group, _):
            first = ((y + SIDE - group) % SIDE) * 2

            @pl.when(core_at == 0)
            def _():
                started(slab_copies(meta, even[:4], even[4:], u_ref, v_ref, first, 2), sems, 16 * first)

            @pl.when(core_at != 0)
            def _():
                started(slab_copies(meta, odd[:4], odd[4:], u_ref, v_ref, first, 2), sems, 16 * first)
            return 0

        for e in range(SIDE):
            near = ((y + SIDE - e) % SIDE) * 2
            for src, k in ((rows[e], near + core_at), (rows[SIDE + e], near + 1 - core_at)):
                pltpu.make_async_copy(src.at[0], ru_ref.at[k], row_sems.at[k]).start()
                pltpu.make_async_copy(src.at[1], rv_ref.at[k], row_sems.at[panels + k]).start()
        lax.fori_loop(0, panels // 2, start_columns, 0)
        waited(four)

        def panel(step, _):
            k = ((y + SIDE - step // 2) % SIDE) * 2 + step % 2

            @pl.when(k % 2 == 0)
            def _():
                waits = slab_copies(meta, odd[:4], odd[4:], u_ref, v_ref, k, 2)
                waited([pltpu.make_async_copy(src, dst, sems.at[16 * k + i]) for i, (src, dst) in enumerate(waits)])
            pltpu.make_async_copy(rows[0].at[0], ru_ref.at[k], row_sems.at[k]).wait()
            pltpu.make_async_copy(rows[0].at[1], rv_ref.at[k], row_sems.at[panels + k]).wait()
            tile_panel(meta, k, tile_ref, u_ref, v_ref, ru_ref, rv_ref)
            rank = meta[4 + k]
            vk = v_ref[k]
            core = masked(tn(vk, vk), rank, rank)
            part = jnp.dot(u_ref[k, at, :], core, preferred_element_type=jnp.float32).astype(jnp.bfloat16)
            slab_ref[...] = slab_ref[...] - nt(part, u_ref[k])
            return 0
        lax.fori_loop(0, panels, panel, 0)
        waited(started([(tile_ref, out_hbm), (slab_ref, dout_hbm)], sems, 0))


def tile_scratch(panels, order, rank):
    stack = pltpu.VMEM((panels, order, rank), jnp.bfloat16)
    return [stack] * 4 + [pltpu.VMEM((order, order), jnp.float32), pltpu.VMEM((64, order), jnp.float32),
                          pltpu.SemaphoreType.DMA((130,)), pltpu.SemaphoreType.DMA((2 * panels,))]


def moved(value, pairs):
    return lax.ppermute(value, AXES, pairs)


def along(axis, step, parity):
    pairs = []
    for x in range(SIDE):
        for z in range(SIDE):
            for col in range(parity, 8, 2):
                to = ((x + step) % SIDE, z) if axis == "x" else (x, (z + step) % SIDE)
                pairs.append(((x * SIDE + z) * 8 + col, (to[0] * SIDE + to[1]) * 8 + col))
    return pairs


def across(change):
    return [(row * 8 + col, row * 8 + change(col)) for row in range(16) for col in range(8)]


def first_leg(first, second, parity):
    a = [first] + [moved(first, along("x", d, parity)) for d in (1, 3, 2)]
    b = [second] + [moved(second, along("z", d, parity)) for d in (1, 3, 2)]
    return a, b


def second_leg(a, b, parity):
    a, b = jnp.stack([a[0], a[1], a[3], a[2]]), jnp.stack([b[0], b[1], b[3], b[2]])
    fs = [a] + [moved(a, along("z", d, parity)) for d in (1, 2, 3)]
    gs = [b] + [moved(b, along("x", d, parity)) for d in (1, 2, 3)]
    return fs, gs


def shards(band, diag, row_factors, row_ranks, col_factors, col_ranks):
    column = lax.axis_index("cols")
    slab = lax.axis_index("rows")
    panels, slab_rows = col_factors.shape[0], diag.shape[1]
    order, rank = row_factors.shape[3], row_factors.shape[4]
    own_ranks = lax.dynamic_index_in_dim(col_ranks, column, 0, keepdims=False)
    meta = jnp.concatenate([jnp.stack([column, slab // SIDE, slab % SIDE, slab]).astype(jnp.int32), own_ranks])

    turned = row_factors[0, 0, 1].reshape(order // rank, rank, rank).transpose(0, 2, 1)
    kept = (jnp.arange(rank, dtype=jnp.int32) < row_ranks[0, 0])[None, :, None]
    turned = jnp.where(kept, turned, jnp.zeros((), turned.dtype)).reshape(order, rank)
    mine = jnp.stack([row_factors[0, 0, 0], turned])

    own = lax.all_to_all(col_factors, "cols", split_axis=0, concat_axis=1, tiled=True)[0]
    pieces = diag[0].reshape(slab_rows, 4, rank).transpose(1, 0, 2)
    rounded = lax.reduce_precision(pieces, exponent_bits=8, mantissa_bits=7)
    high = rounded.astype(jnp.bfloat16)
    low = (pieces - rounded).astype(jnp.bfloat16)
    own, mine, meta, high, low = lax.optimization_barrier((own, mine, meta, high, low))
    near = [mine] + [moved(mine, across(lambda c, d=d: ((c // 2 + d) % SIDE) * 2 + c % 2)) for d in (1, 2, 3)]
    sides, bases = own[:, 1], own[:, 0]
    a, b = lax.optimization_barrier(first_leg(jnp.concatenate([sides, high]), jnp.concatenate([bases, low]), 0))
    fs, gs = second_leg(a, b, 0)
    far = [moved(p, across(lambda c: c ^ 1)) for p in near]
    odd_a, odd_b = lax.optimization_barrier(first_leg(sides, bases, 1))
    odd_fs, odd_gs = second_leg(odd_a, odd_b, 1)
    fs, gs, near, far, own_a, own_b = lax.optimization_barrier((fs, gs, near, far, odd_fs[0], odd_gs[0]))
    odd_fs, odd_gs = [own_a] + odd_fs[1:], [own_b] + odd_gs[1:]

    hbm = pl.BlockSpec(memory_space=pl.ANY)
    smem = pl.BlockSpec(memory_space=pltpu.SMEM)
    outs = (jax.ShapeDtypeStruct((order, order), jnp.float32), jax.ShapeDtypeStruct((slab_rows, order), jnp.float32))
    params = pltpu.CompilerParams(vmem_limit_bytes=60 << 20)
    tile, slab_out = pl.pallas_call(
        column_kernel,
        out_shape=outs,
        in_specs=[smem] + [hbm] * 17,
        out_specs=(hbm, hbm),
        scratch_shapes=column_scratch(panels, order, rank),
        cost_estimate=pl.CostEstimate(flops=60_000_000_000, bytes_accessed=20_000_000, transcendentals=0),
        compiler_params=params, name="column")(meta, *fs, *gs, *near, *far, band[0, 0])

    tile, slab_out = pl.pallas_call(
        tile_kernel,
        out_shape=outs,
        in_specs=[smem] + [hbm] * 28,
        out_specs=(hbm, hbm),
        scratch_shapes=tile_scratch(panels, order, rank),
        input_output_aliases={27: 0, 28: 1},
        cost_estimate=pl.CostEstimate(flops=10_000_000_000, bytes_accessed=40_000_000, transcendentals=0),
        compiler_params=params, name="tile")(
            meta, *fs, *gs, *odd_fs, *odd_gs, *near, *far, band[0, 0], diag[0], tile, slab_out)
    return tile[None, None], slab_out[None]


def solution(mesh):
    placed = (
        P("rows", "cols", None, None),
        P("cols", "rows", None),
        P("rows", "cols", None, None, None),
        P("rows", "cols"),
        P(None, "cols", None, "rows", None),
        P(),
    )
    return jax.shard_map(
        shards,
        mesh=mesh,
        in_specs=placed,
        out_specs=(P("rows", "cols", None, None), P("cols", "rows", None)),
        check_vma=False,
    )
```

```python
import jax
import jax.numpy as jnp
from jax import lax
from jax.experimental import pallas as pl
from jax.experimental.pallas import tpu as pltpu
from jax.sharding import PartitionSpec as P


NB = 128
G = 8
SIDE = 4
AXES = ("rows", "cols")
COLUMN_GRANT = 46 << 20
TILE_GRANT = 60 << 20


def split2(x):
    hi = x.astype(jnp.bfloat16)
    lo = (x - hi.astype(jnp.float32)).astype(jnp.bfloat16)
    return hi, lo


def nt(a, b):
    return lax.dot_general(a, b, (((1,), (1,)), ((), ())), preferred_element_type=jnp.float32)


def nt3(ah, al, bh, bl):
    return nt(jnp.concatenate([ah, al, ah], axis=1), jnp.concatenate([bh, bh, bl], axis=1))


def lane_splat(x, lane):
    return jnp.broadcast_to(x[:, lane:lane + 1], x.shape)


def row_splat(x, s):
    return jnp.broadcast_to(x[s:s + 1, :], x.shape)


def factor_block(t_ref, up_ref, one_ref):
    one = one_ref[...]
    sub = lax.broadcasted_iota(jnp.int32, (G, NB), 0)
    lane = lax.broadcasted_iota(jnp.int32, (G, NB), 1)
    count = NB // G
    first = t_ref[0:G, :]
    diag = [lane_splat(first, c) * one for c in range(G)]
    for g in range(count):
        base = g * G
        v = t_ref[base:base + G, :]
        b = [[row_splat(diag[j], s) if s >= j else None for j in range(G)] for s in range(G)]
        more = g + 1 < count
        if more:
            below = t_ref[base + G:base + 2 * G, :]
            wn = [lane_splat(below, base + j) for j in range(G)]
            diag = [lane_splat(below, base + G + c) for c in range(G)]
        inside = (lane >= base) & (lane < base + G)
        vi = jnp.where(inside, jnp.where(lane - base == sub, 1.0, 0.0), v)
        low = [[None] * G for _ in range(G)]
        rinv = [None] * G
        ra = [row_splat(v, s) for s in range(G)]
        r = [row_splat(vi, s) for s in range(G)]
        for j in range(G):
            rinv[j] = lax.rsqrt(b[j][j])
            for s in range(j + 1, G):
                low[s][j] = b[s][j] * rinv[j]
            for t in range(j + 1, G):
                for s in range(t, G):
                    b[s][t] = b[s][t] - low[s][j] * low[t][j]
            if more:
                ln = wn[j] * rinv[j]
                for t in range(j + 1, G):
                    wn[t] = wn[t] - ln * low[t][j]
                for c in range(G):
                    diag[c] = diag[c] - ln * row_splat(ln, c)
            ra[j] = ra[j] * rinv[j]
            r[j] = r[j] * rinv[j]
            for s in range(j + 1, G):
                ra[s] = ra[s] - low[s][j] * ra[j]
                r[s] = r[s] - low[s][j] * r[j]
        out, outa = r[0], ra[0]
        for s in range(1, G):
            out = jnp.where(sub == s, r[s], out)
            outa = jnp.where(sub == s, ra[s], outa)
        up_ref[base:base + G, :] = outa
        t_ref[base:base + G, :] = out
        if more:
            m = [None] * G
            for s in reversed(range(G)):
                acc = r[s]
                for t in range(s + 1, G):
                    acc = acc - low[t][s] * m[t]
                m[s] = acc * rinv[s]
            for rb in range(g + 1, count):
                w = t_ref[rb * G:(rb + 1) * G, :]
                acc = jnp.where(inside, 0.0, w)
                for j in range(G):
                    acc = acc - lane_splat(w, base + j) * m[j]
                t_ref[rb * G:(rb + 1) * G, :] = acc


def chol_body(a_ref, inv_ref, t_ref, up_ref, one_ref, beside):
    n = a_ref.shape[0]
    nblk = n // NB
    ri = lax.broadcasted_iota(jnp.int32, (NB, NB), 0)
    ci = lax.broadcasted_iota(jnp.int32, (NB, NB), 1)

    def step(j, _):
        o = pl.multiple_of(j * NB, NB)
        t_ref[...] = a_ref[pl.ds(o, NB), pl.ds(o, NB)]
        factor_block(t_ref, up_ref, one_ref)
        beside(j)
        inv = jnp.where(ri >= ci, t_ref[...], 0.0)
        inv_ref[pl.ds(o, NB), :] = inv
        low = jnp.where(ri >= ci, up_ref[...].T, 0.0)
        ih, il = split2(inv)
        for v in range(nblk // 2):
            lo_row = 2 * NB * v

            @pl.when((j + 1) // 2 == v)
            def _():
                p = a_ref[lo_row:, pl.ds(o, NB)]
                ph, plo = split2(p)
                x = nt3(ph, plo, ih, il)
                rows = lax.broadcasted_iota(jnp.int32, x.shape, 0) + lo_row
                x = jnp.where(rows >= o + NB, x, 0.0)
                a_ref[lo_row:, pl.ds(o, NB)] = x
                xh, xl = split2(x)
                c = nt3(xh, xl, xh, xl)
                a_ref[lo_row:, lo_row:] = a_ref[lo_row:, lo_row:] - c
        a_ref[pl.ds(o, NB), pl.ds(o, NB)] = low
        return 0

    lax.fori_loop(0, nblk, step, 0)


def solve_body(b_ref, l_ref, inv_ref, x_ref, xh_ref, xl_ref, done):
    n = b_ref.shape[0]
    for j in range(n // (2 * NB)):
        o = 2 * NB * j
        s = slice(o, o + 2 * NB)
        i0, i1 = inv_ref[o:o + NB, :], inv_ref[o + NB:o + 2 * NB, :]
        i0h, i0l = split2(i0.T)
        i1h, i1l = split2(i1)
        mh, ml = split2(nt3(*split2(l_ref[o + NB:o + 2 * NB, o:o + NB]), i0h, i0l))
        off = -nt3(i1h, i1l, *split2(nt_same(mh, ml)))
        inv = jnp.concatenate([jnp.concatenate([i0, jnp.zeros_like(i0)], axis=1), jnp.concatenate([off, i1], axis=1)], axis=0)
        ih, il = split2(inv)
        acc = b_ref[:, s]
        if j:
            lh, ll = split2(l_ref[s, :o])
            acc = acc - nt(xh_ref[:, :o], lh) - nt(xl_ref[:, :o], lh) - nt(xh_ref[:, :o], ll)
        ah, al = split2(acc)
        x = nt3(ah, al, ih, il)
        x_ref[:, s] = x
        done(j, s)
        xh, xl = split2(x)
        xh_ref[:, s] = xh
        xl_ref[:, s] = xl


def nt_same(mh, ml):
    return (mh.astype(jnp.float32) + ml.astype(jnp.float32)).T


def tn(a, b):
    return lax.dot_general(a, b, (((0,), (0,)), ((), ())), preferred_element_type=jnp.float32)


def masked(core, rank_a, rank_b):
    kept = lax.broadcasted_iota(jnp.int32, core.shape, 1) < rank_b
    if rank_a is not None:
        kept = kept & (lax.broadcasted_iota(jnp.int32, core.shape, 0) < rank_a)
    return jnp.where(kept, core, 0.0).astype(jnp.bfloat16)


def started(pairs, sems, first=0):
    copies = [pltpu.make_async_copy(src, dst, sems.at[first + n]) for n, (src, dst) in enumerate(pairs)]
    for copy in copies:
        copy.start()
    return copies


def waited(copies):
    for copy in copies:
        copy.wait()


def slab_copies(meta, fs, gs, u_ref, v_ref, first, count, to=None):
    x, z = meta[1], meta[2]
    pairs = []
    for e in range(SIDE):
        for d in range(SIDE):
            slab = ((x + SIDE - d) % SIDE) * SIDE + (z + SIDE - e) % SIDE
            at = pl.ds(pl.multiple_of(slab * 64, 64), 64)
            pairs.append((fs[e].at[d, pl.ds(first, count)], v_ref.at[pl.ds(first if to is None else to, count), at, :]))
            pairs.append((gs[d].at[e, pl.ds(first, count)], u_ref.at[pl.ds(first if to is None else to, count), at, :]))
    return pairs


def row_copies(meta, rows, ru_ref, rv_ref):
    y, core_at = meta[0] // 2, meta[0] % 2
    pairs = []
    for e in range(SIDE):
        near = ((y + SIDE - e) % SIDE) * 2
        for src, k in ((rows[e], near + core_at), (rows[SIDE + e], near + 1 - core_at)):
            pairs.append((src.at[0], ru_ref.at[k]))
            pairs.append((src.at[1], rv_ref.at[k]))
    return pairs


def tile_panel(meta, k, tile_ref, u_ref, v_ref, ru_ref, rv_ref):
    n = tile_ref.shape[0]
    core = jnp.dot(rv_ref[k, 0:256], v_ref[k, 0:256], preferred_element_type=jnp.float32)
    for q in range(256, n, 256):
        core = core + jnp.dot(rv_ref[k, q:q + 256], v_ref[k, q:q + 256], preferred_element_type=jnp.float32)
    core = masked(core, None, meta[4 + k])
    left = jnp.dot(ru_ref[k], core, preferred_element_type=jnp.float32).astype(jnp.bfloat16)
    uk = u_ref[k]
    for s in range(0, n, 512):
        tile_ref[s:s + 512, :] = tile_ref[s:s + 512, :] - nt(left[s:s + 512], uk)


def column_kernel(meta, *refs):
    fs, gs, rows = refs[0:4], refs[4:8], refs[8:16]
    band_hbm, out_hbm, dout_hbm = refs[16:19]
    (u_ref, v_ref, hi_ref, lo_ref, ru_ref, rv_ref, tile_ref, acc_ref, l_ref, inv_ref, t_ref, up_ref, one_ref, xh_ref, xl_ref, sems) = refs[19:]
    n = l_ref.shape[0]

    @pl.when(meta[0] == 0)
    def _():
        one = started(slab_copies(meta, fs, gs, u_ref, v_ref, 0, 4), sems, 0)
        two = started(slab_copies(meta, fs, gs, u_ref, v_ref, 4, 4), sems, 32)
        three = started(slab_copies(meta, fs, gs, lo_ref, hi_ref, 8, 4, 0), sems, 64)
        acc_ref[...] = jnp.zeros_like(acc_ref)

        four = [pltpu.make_async_copy(src, dst, sems.at[96 + n])
                for n, (src, dst) in enumerate(row_copies(meta, rows, ru_ref, rv_ref) + [(band_hbm, tile_ref)])]

        def panel(k, _):
            @pl.when(k == 4)
            def _():
                waited(two)
                for copy in four:
                    copy.start()

            rank = meta[4 + k]
            vk, uk = v_ref[k], u_ref[k]
            core = masked(tn(vk, vk), rank, rank)
            left = jnp.dot(uk, core, preferred_element_type=jnp.float32).astype(jnp.bfloat16)
            for s in range(0, n, 512):
                acc_ref[s:s + 512, :] = acc_ref[s:s + 512, :] - nt(left[s:s + 512], uk)
            return 0

        waited(one)
        lax.fori_loop(0, 8, panel, 0)
        waited(three)

        def whole(rows, cols):
            q, at = cols.start // 256, slice(cols.start % 256, cols.start % 256 + NB)
            return acc_ref[rows, cols] + (hi_ref[q, rows, at].astype(jnp.float32) + lo_ref[q, rows, at].astype(jnp.float32))

        for i in range(n // NB):
            si = slice(i * NB, (i + 1) * NB)
            for j in range(i + 1):
                sj = slice(j * NB, (j + 1) * NB)
                l_ref[si, sj] = (whole(si, sj) + whole(sj, si).T) * 0.5
        waited(four)
        one_ref[...] = jnp.ones_like(one_ref)
        chol_body(l_ref, inv_ref, t_ref, up_ref, one_ref, lambda j: tile_panel(meta, j, tile_ref, u_ref, v_ref, ru_ref, rv_ref))
        for j in range(n // NB - 1):
            l_ref[j * NB:(j + 1) * NB, (j + 1) * NB:] = jnp.zeros((NB, n - (j + 1) * NB), jnp.float32)
        last = started([(l_ref.at[pl.ds(pl.multiple_of(meta[3] * 64, 64), 64), :], dout_hbm)], sems, 0)

        def done(j, s):
            last.extend(started([(tile_ref.at[:, s], out_hbm.at[:, s])], sems, 1 + j))

        solve_body(tile_ref, l_ref, inv_ref, tile_ref, xh_ref, xl_ref, done)
        waited(last)


def column_scratch(panels, order, rank):
    stack = pltpu.VMEM((panels, order, rank), jnp.bfloat16)
    quarter = pltpu.VMEM((4, order, rank), jnp.bfloat16)
    square = pltpu.VMEM((order, order), jnp.float32)
    block = pltpu.VMEM((NB, NB), jnp.float32)
    return [stack, stack, quarter, quarter, stack, stack, square, square, square,
            pltpu.VMEM((order, NB), jnp.float32), block, block, pltpu.VMEM((G, NB), jnp.float32),
            pltpu.VMEM((order, order), jnp.bfloat16), pltpu.VMEM((order, order), jnp.bfloat16),
            pltpu.SemaphoreType.DMA((128,))]


def tile_kernel(meta, *refs):
    even, odd, rows = refs[0:8], refs[8:16], refs[16:24]
    band_hbm, diag_hbm, _, _, out_hbm, dout_hbm = refs[24:30]
    u_ref, v_ref, ru_ref, rv_ref, tile_ref, slab_ref, sems, row_sems = refs[30:]
    panels = u_ref.shape[0]
    at = pl.ds(pl.multiple_of(meta[3] * 64, 64), 64)
    y, core_at = meta[0] // 2, meta[0] % 2

    @pl.when(meta[0] != 0)
    def _():
        four = started([(band_hbm, tile_ref), (diag_hbm, slab_ref)], sems, 128)

        def start_columns(group, _):
            first = ((y + SIDE - group) % SIDE) * 2

            @pl.when(core_at == 0)
            def _():
                started(slab_copies(meta, even[:4], even[4:], u_ref, v_ref, first, 2), sems, 16 * first)

            @pl.when(core_at != 0)
            def _():
                started(slab_copies(meta, odd[:4], odd[4:], u_ref, v_ref, first, 2), sems, 16 * first)

            return 0

        for e in range(SIDE):
            near = ((y + SIDE - e) % SIDE) * 2
            for src, k in ((rows[e], near + core_at), (rows[SIDE + e], near + 1 - core_at)):
                pltpu.make_async_copy(src.at[0], ru_ref.at[k], row_sems.at[k]).start()
                pltpu.make_async_copy(src.at[1], rv_ref.at[k], row_sems.at[panels + k]).start()
        lax.fori_loop(0, panels // 2, start_columns, 0)
        waited(four)

        def panel(step, _):
            k = ((y + SIDE - step // 2) % SIDE) * 2 + step % 2

            @pl.when(k % 2 == 0)
            def _():
                waits = slab_copies(meta, odd[:4], odd[4:], u_ref, v_ref, k, 2)
                waited([pltpu.make_async_copy(src, dst, sems.at[16 * k + i]) for i, (src, dst) in enumerate(waits)])

            pltpu.make_async_copy(rows[0].at[0], ru_ref.at[k], row_sems.at[k]).wait()
            pltpu.make_async_copy(rows[0].at[1], rv_ref.at[k], row_sems.at[panels + k]).wait()
            tile_panel(meta, k, tile_ref, u_ref, v_ref, ru_ref, rv_ref)
            rank = meta[4 + k]
            vk = v_ref[k]
            core = masked(tn(vk, vk), rank, rank)
            part = jnp.dot(u_ref[k, at, :], core, preferred_element_type=jnp.float32).astype(jnp.bfloat16)
            slab_ref[...] = slab_ref[...] - nt(part, u_ref[k])
            return 0

        lax.fori_loop(0, panels, panel, 0)
        waited(started([(tile_ref, out_hbm), (slab_ref, dout_hbm)], sems, 0))


def tile_scratch(panels, order, rank):
    stack = pltpu.VMEM((panels, order, rank), jnp.bfloat16)
    return [stack] * 4 + [pltpu.VMEM((order, order), jnp.float32), pltpu.VMEM((64, order), jnp.float32),
                          pltpu.SemaphoreType.DMA((130,)), pltpu.SemaphoreType.DMA((2 * panels,))]


def moved(value, pairs):
    return lax.ppermute(value, AXES, pairs)


def along(axis, step, parity):
    pairs = []
    for x in range(SIDE):
        for z in range(SIDE):
            for col in range(parity, 8, 2):
                to = ((x + step) % SIDE, z) if axis == "x" else (x, (z + step) % SIDE)
                pairs.append(((x * SIDE + z) * 8 + col, (to[0] * SIDE + to[1]) * 8 + col))
    return pairs


def across(change):
    return [(row * 8 + col, row * 8 + change(col)) for row in range(16) for col in range(8)]


def both_ways(a, b, one, two, parity):
    got_a, got_b = [a, None, None, None], [b, None, None, None]
    for d in (1, 3, 2):
        got_a[d] = moved(a, along(one, d, parity))
        got_b[d] = moved(b, along(two, d, parity))
    return got_a, got_b


def first_leg(first, second, parity):
    return both_ways(first, second, "x", "z", parity)


def second_leg(a, b, parity):
    a, b = lax.optimization_barrier((jnp.stack(a), jnp.stack(b)))
    return both_ways(a, b, "z", "x", parity)


def shards(band, diag, row_factors, row_ranks, col_factors, col_ranks):
    column = lax.axis_index("cols")
    slab = lax.axis_index("rows")
    panels, slab_rows = col_factors.shape[0], diag.shape[1]
    order, rank = row_factors.shape[3], row_factors.shape[4]
    own_ranks = lax.dynamic_index_in_dim(col_ranks, column, 0, keepdims=False)
    meta = jnp.concatenate([jnp.stack([column, slab // SIDE, slab % SIDE, slab]).astype(jnp.int32), own_ranks])

    turned = row_factors[0, 0, 1].reshape(order // rank, rank, rank).transpose(0, 2, 1)
    kept = (jnp.arange(rank, dtype=jnp.int32) < row_ranks[0, 0])[None, :, None]
    turned = jnp.where(kept, turned, jnp.zeros((), turned.dtype)).reshape(order, rank)
    mine = jnp.stack([row_factors[0, 0, 0], turned])

    own = lax.all_to_all(col_factors, "cols", split_axis=0, concat_axis=1, tiled=True)[0]
    pieces = diag[0].reshape(slab_rows, 4, rank).transpose(1, 0, 2)
    rounded = lax.reduce_precision(pieces, exponent_bits=8, mantissa_bits=7)
    high = rounded.astype(jnp.bfloat16)
    low = (pieces - rounded).astype(jnp.bfloat16)
    own, mine, meta, high, low = lax.optimization_barrier((own, mine, meta, high, low))
    near = [mine] + [moved(mine, across(lambda c, d=d: ((c // 2 + d) % SIDE) * 2 + c % 2)) for d in (1, 2, 3)]
    sides, bases = own[:, 1], own[:, 0]
    a, b = lax.optimization_barrier(first_leg(jnp.concatenate([sides, high]), jnp.concatenate([bases, low]), 0))
    fs, gs = second_leg(a, b, 0)
    far = [moved(p, across(lambda c: c ^ 1)) for p in near]
    odd_a, odd_b = lax.optimization_barrier(first_leg(sides, bases, 1))
    odd_fs, odd_gs = second_leg(odd_a, odd_b, 1)
    fs, gs, near, far, own_a, own_b = lax.optimization_barrier((fs, gs, near, far, odd_fs[0], odd_gs[0]))
    odd_fs, odd_gs = [own_a] + odd_fs[1:], [own_b] + odd_gs[1:]

    hbm = pl.BlockSpec(memory_space=pl.ANY)
    smem = pl.BlockSpec(memory_space=pltpu.SMEM)
    outs = (jax.ShapeDtypeStruct((order, order), jnp.float32), jax.ShapeDtypeStruct((slab_rows, order), jnp.float32))
    params = pltpu.CompilerParams(vmem_limit_bytes=COLUMN_GRANT)
    tile, slab_out = pl.pallas_call(
        column_kernel,
        out_shape=outs,
        in_specs=[smem] + [hbm] * 17,
        out_specs=(hbm, hbm),
        scratch_shapes=column_scratch(panels, order, rank),
        cost_estimate=pl.CostEstimate(flops=60_000_000_000, bytes_accessed=20_000_000, transcendentals=0),
        compiler_params=params, name="column")(meta, *fs, *gs, *near, *far, band[0, 0])

    tile, slab_out = pl.pallas_call(
        tile_kernel,
        out_shape=outs,
        in_specs=[smem] + [hbm] * 28,
        out_specs=(hbm, hbm),
        scratch_shapes=tile_scratch(panels, order, rank),
        input_output_aliases={27: 0, 28: 1},
        cost_estimate=pl.CostEstimate(flops=10_000_000_000, bytes_accessed=40_000_000, transcendentals=0),
        compiler_params=pltpu.CompilerParams(vmem_limit_bytes=TILE_GRANT), name="tile")(
            meta, *fs, *gs, *odd_fs, *odd_gs, *near, *far, band[0, 0], diag[0], tile, slab_out)
    return tile[None, None], slab_out[None]


def solution(mesh):
    placed = (
        P("rows", "cols", None, None),
        P("cols", "rows", None),
        P("rows", "cols", None, None, None),
        P("rows", "cols"),
        P(None, "cols", None, "rows", None),
        P(),
    )
    return jax.shard_map(
        shards,
        mesh=mesh,
        in_specs=placed,
        out_specs=(P("rows", "cols", None, None), P("cols", "rows", None)),
        check_vma=False,
    )
```

```python
import jax
import jax.numpy as jnp
from jax import lax
from jax.experimental import pallas as pl
from jax.experimental.pallas import tpu as pltpu
from jax.sharding import PartitionSpec as P


NB = 128
G = 8
SIDE = 4
AXES = ("rows", "cols")
NEAR = (0, 1, 3, 2)
COLUMN_GRANT = 46 << 20
TILE_GRANT = 60 << 20


def split2(x):
    hi = x.astype(jnp.bfloat16)
    lo = (x - hi.astype(jnp.float32)).astype(jnp.bfloat16)
    return hi, lo


def nt(a, b):
    return lax.dot_general(a, b, (((1,), (1,)), ((), ())), preferred_element_type=jnp.float32)


def nt3(ah, al, bh, bl):
    return nt(jnp.concatenate([ah, al, ah], axis=1), jnp.concatenate([bh, bh, bl], axis=1))


def lane_splat(x, lane):
    return jnp.broadcast_to(x[:, lane:lane + 1], x.shape)


def row_splat(x, s):
    return jnp.broadcast_to(x[s:s + 1, :], x.shape)


def factor_block(t_ref, up_ref, one_ref):
    one = one_ref[...]
    sub = lax.broadcasted_iota(jnp.int32, (G, NB), 0)
    lane = lax.broadcasted_iota(jnp.int32, (G, NB), 1)
    count = NB // G
    first = t_ref[0:G, :]
    diag = [lane_splat(first, c) * one for c in range(G)]
    for g in range(count):
        base = g * G
        v = t_ref[base:base + G, :]
        b = [[row_splat(diag[j], s) if s >= j else None for j in range(G)] for s in range(G)]
        more = g + 1 < count
        if more:
            below = t_ref[base + G:base + 2 * G, :]
            wn = [lane_splat(below, base + j) for j in range(G)]
            diag = [lane_splat(below, base + G + c) for c in range(G)]
        inside = (lane >= base) & (lane < base + G)
        vi = jnp.where(inside, jnp.where(lane - base == sub, 1.0, 0.0), v)
        low = [[None] * G for _ in range(G)]
        rinv = [None] * G
        ra = [row_splat(v, s) for s in range(G)]
        r = [row_splat(vi, s) for s in range(G)]
        for j in range(G):
            rinv[j] = lax.rsqrt(b[j][j])
            for s in range(j + 1, G):
                low[s][j] = b[s][j] * rinv[j]
            for t in range(j + 1, G):
                for s in range(t, G):
                    b[s][t] = b[s][t] - low[s][j] * low[t][j]
            if more:
                ln = wn[j] * rinv[j]
                for t in range(j + 1, G):
                    wn[t] = wn[t] - ln * low[t][j]
                for c in range(G):
                    diag[c] = diag[c] - ln * row_splat(ln, c)
            ra[j] = ra[j] * rinv[j]
            r[j] = r[j] * rinv[j]
            for s in range(j + 1, G):
                ra[s] = ra[s] - low[s][j] * ra[j]
                r[s] = r[s] - low[s][j] * r[j]
        out, outa = r[0], ra[0]
        for s in range(1, G):
            out = jnp.where(sub == s, r[s], out)
            outa = jnp.where(sub == s, ra[s], outa)
        up_ref[base:base + G, :] = outa
        t_ref[base:base + G, :] = out
        if more:
            m = [None] * G
            for s in reversed(range(G)):
                acc = r[s]
                for t in range(s + 1, G):
                    acc = acc - low[t][s] * m[t]
                m[s] = acc * rinv[s]
            for rb in range(g + 1, count):
                w = t_ref[rb * G:(rb + 1) * G, :]
                acc = jnp.where(inside, 0.0, w)
                for j in range(G):
                    acc = acc - lane_splat(w, base + j) * m[j]
                t_ref[rb * G:(rb + 1) * G, :] = acc


def chol_body(a_ref, inv_ref, t_ref, up_ref, one_ref, beside):
    n = a_ref.shape[0]
    nblk = n // NB
    ri = lax.broadcasted_iota(jnp.int32, (NB, NB), 0)
    ci = lax.broadcasted_iota(jnp.int32, (NB, NB), 1)

    def step(j, _):
        o = pl.multiple_of(j * NB, NB)
        t_ref[...] = a_ref[pl.ds(o, NB), pl.ds(o, NB)]
        factor_block(t_ref, up_ref, one_ref)
        beside(j)
        inv = jnp.where(ri >= ci, t_ref[...], 0.0)
        inv_ref[pl.ds(o, NB), :] = inv
        low = jnp.where(ri >= ci, up_ref[...].T, 0.0)
        ih, il = split2(inv)
        for v in range(nblk // 2):
            lo_row = 2 * NB * v

            @pl.when((j + 1) // 2 == v)
            def _():
                p = a_ref[lo_row:, pl.ds(o, NB)]
                ph, plo = split2(p)
                x = nt3(ph, plo, ih, il)
                rows = lax.broadcasted_iota(jnp.int32, x.shape, 0) + lo_row
                x = jnp.where(rows >= o + NB, x, 0.0)
                a_ref[lo_row:, pl.ds(o, NB)] = x
                xh, xl = split2(x)
                c = nt3(xh, xl, xh, xl)
                a_ref[lo_row:, lo_row:] = a_ref[lo_row:, lo_row:] - c
        a_ref[pl.ds(o, NB), pl.ds(o, NB)] = low
        return 0

    lax.fori_loop(0, nblk, step, 0)


def solve_body(b_ref, l_ref, inv_ref, x_ref, xh_ref, xl_ref, done):
    n = b_ref.shape[0]
    for j in range(n // (2 * NB)):
        o = 2 * NB * j
        s = slice(o, o + 2 * NB)
        i0, i1 = inv_ref[o:o + NB, :], inv_ref[o + NB:o + 2 * NB, :]
        i0h, i0l = split2(i0.T)
        i1h, i1l = split2(i1)
        mh, ml = split2(nt3(*split2(l_ref[o + NB:o + 2 * NB, o:o + NB]), i0h, i0l))
        off = -nt3(i1h, i1l, *split2(nt_same(mh, ml)))
        inv = jnp.concatenate([jnp.concatenate([i0, jnp.zeros_like(i0)], axis=1), jnp.concatenate([off, i1], axis=1)], axis=0)
        ih, il = split2(inv)
        acc = b_ref[:, s]
        if j:
            lh, ll = split2(l_ref[s, :o])
            acc = acc - nt(xh_ref[:, :o], lh) - nt(xl_ref[:, :o], lh) - nt(xh_ref[:, :o], ll)
        ah, al = split2(acc)
        x = nt3(ah, al, ih, il)
        x_ref[:, s] = x
        done(j, s)
        xh, xl = split2(x)
        xh_ref[:, s] = xh
        xl_ref[:, s] = xl


def nt_same(mh, ml):
    return (mh.astype(jnp.float32) + ml.astype(jnp.float32)).T


def tn(a, b):
    return lax.dot_general(a, b, (((0,), (0,)), ((), ())), preferred_element_type=jnp.float32)


def masked(core, rank_a, rank_b):
    kept = lax.broadcasted_iota(jnp.int32, core.shape, 1) < rank_b
    if rank_a is not None:
        kept = kept & (lax.broadcasted_iota(jnp.int32, core.shape, 0) < rank_a)
    return jnp.where(kept, core, 0.0).astype(jnp.bfloat16)


def started(pairs, sems, first=0):
    copies = [pltpu.make_async_copy(src, dst, sems.at[first + n]) for n, (src, dst) in enumerate(pairs)]
    for copy in copies:
        copy.start()
    return copies


def waited(copies):
    for copy in copies:
        copy.wait()


def slab_copies(meta, fs, gs, u_ref, v_ref, first, count, to=None):
    x, z = meta[1], meta[2]
    pairs = []
    for e in range(SIDE):
        for d in range(SIDE):
            for far, near, at_x, at_z, dst in (
                (e, d, x ^ NEAR[d], (z + SIDE - e) % SIDE, v_ref), (d, e, (x + SIDE - d) % SIDE, z ^ NEAR[e], u_ref)
            ):
                at = pl.ds(pl.multiple_of((at_x * SIDE + at_z) * 64, 64), 64)
                src = fs[far] if dst is v_ref else gs[far]
                pairs.append((src.at[near, pl.ds(first, count)], dst.at[pl.ds(first if to is None else to, count), at, :]))
    return pairs


def row_copies(meta, rows, ru_ref, rv_ref):
    y, core_at = meta[0] // 2, meta[0] % 2
    pairs = []
    for e in range(SIDE):
        near = ((y + SIDE - e) % SIDE) * 2
        for src, k in ((rows[e], near + core_at), (rows[SIDE + e], near + 1 - core_at)):
            pairs.append((src.at[0], ru_ref.at[k]))
            pairs.append((src.at[1], rv_ref.at[k]))
    return pairs


def tile_panel(meta, k, tile_ref, u_ref, v_ref, ru_ref, rv_ref):
    n = tile_ref.shape[0]
    core = jnp.dot(rv_ref[k, 0:256], v_ref[k, 0:256], preferred_element_type=jnp.float32)
    for q in range(256, n, 256):
        core = core + jnp.dot(rv_ref[k, q:q + 256], v_ref[k, q:q + 256], preferred_element_type=jnp.float32)
    core = masked(core, None, meta[4 + k])
    left = jnp.dot(ru_ref[k], core, preferred_element_type=jnp.float32).astype(jnp.bfloat16)
    uk = u_ref[k]
    for s in range(0, n, 512):
        tile_ref[s:s + 512, :] = tile_ref[s:s + 512, :] - nt(left[s:s + 512], uk)


def column_kernel(meta, *refs):
    fs, gs, rows = refs[0:4], refs[4:8], refs[8:16]
    band_hbm, out_hbm, dout_hbm = refs[16:19]
    (u_ref, v_ref, hi_ref, lo_ref, ru_ref, rv_ref, tile_ref, acc_ref, l_ref, inv_ref, t_ref, up_ref, one_ref, xh_ref, xl_ref, sems) = refs[19:]
    n = l_ref.shape[0]

    @pl.when(meta[0] == 0)
    def _():
        one = started(slab_copies(meta, fs, gs, u_ref, v_ref, 0, 4), sems, 0)
        two = started(slab_copies(meta, fs, gs, u_ref, v_ref, 4, 4), sems, 32)
        three = started(slab_copies(meta, fs, gs, lo_ref, hi_ref, 8, 4, 0), sems, 64)
        acc_ref[...] = jnp.zeros_like(acc_ref)

        four = [pltpu.make_async_copy(src, dst, sems.at[96 + n])
                for n, (src, dst) in enumerate(row_copies(meta, rows, ru_ref, rv_ref) + [(band_hbm, tile_ref)])]

        def panel(k, _):
            @pl.when(k == 4)
            def _():
                waited(two)
                for copy in four:
                    copy.start()

            rank = meta[4 + k]
            vk, uk = v_ref[k], u_ref[k]
            core = masked(tn(vk, vk), rank, rank)
            left = jnp.dot(uk, core, preferred_element_type=jnp.float32).astype(jnp.bfloat16)
            for s in range(0, n, 512):
                acc_ref[s:s + 512, :] = acc_ref[s:s + 512, :] - nt(left[s:s + 512], uk)
            return 0

        waited(one)
        lax.fori_loop(0, 8, panel, 0)
        waited(three)

        def whole(rows, cols):
            q, at = cols.start // 256, slice(cols.start % 256, cols.start % 256 + NB)
            return acc_ref[rows, cols] + (hi_ref[q, rows, at].astype(jnp.float32) + lo_ref[q, rows, at].astype(jnp.float32))

        for i in range(n // NB):
            si = slice(i * NB, (i + 1) * NB)
            for j in range(i + 1):
                sj = slice(j * NB, (j + 1) * NB)
                l_ref[si, sj] = (whole(si, sj) + whole(sj, si).T) * 0.5
        waited(four)
        one_ref[...] = jnp.ones_like(one_ref)
        chol_body(l_ref, inv_ref, t_ref, up_ref, one_ref, lambda j: tile_panel(meta, j, tile_ref, u_ref, v_ref, ru_ref, rv_ref))
        for j in range(n // NB - 1):
            l_ref[j * NB:(j + 1) * NB, (j + 1) * NB:] = jnp.zeros((NB, n - (j + 1) * NB), jnp.float32)
        last = started([(l_ref.at[pl.ds(pl.multiple_of(meta[3] * 64, 64), 64), :], dout_hbm)], sems, 0)

        def done(j, s):
            last.extend(started([(tile_ref.at[:, s], out_hbm.at[:, s])], sems, 1 + j))

        solve_body(tile_ref, l_ref, inv_ref, tile_ref, xh_ref, xl_ref, done)
        waited(last)


def column_scratch(panels, order, rank):
    stack = pltpu.VMEM((panels, order, rank), jnp.bfloat16)
    quarter = pltpu.VMEM((4, order, rank), jnp.bfloat16)
    square = pltpu.VMEM((order, order), jnp.float32)
    block = pltpu.VMEM((NB, NB), jnp.float32)
    return [stack, stack, quarter, quarter, stack, stack, square, square, square,
            pltpu.VMEM((order, NB), jnp.float32), block, block, pltpu.VMEM((G, NB), jnp.float32),
            pltpu.VMEM((order, order), jnp.bfloat16), pltpu.VMEM((order, order), jnp.bfloat16),
            pltpu.SemaphoreType.DMA((128,))]


def tile_kernel(meta, *refs):
    even, odd, rows = refs[0:8], refs[8:16], refs[16:24]
    band_hbm, diag_hbm, _, _, out_hbm, dout_hbm = refs[24:30]
    u_ref, v_ref, ru_ref, rv_ref, tile_ref, slab_ref, sems, row_sems = refs[30:]
    panels = u_ref.shape[0]
    at = pl.ds(pl.multiple_of(meta[3] * 64, 64), 64)
    y, core_at = meta[0] // 2, meta[0] % 2

    @pl.when(meta[0] != 0)
    def _():
        four = started([(band_hbm, tile_ref), (diag_hbm, slab_ref)], sems, 128)

        def start_columns(group, _):
            first = ((y + SIDE - group) % SIDE) * 2

            @pl.when(core_at == 0)
            def _():
                started(slab_copies(meta, even[:4], even[4:], u_ref, v_ref, first, 2), sems, 16 * first)

            @pl.when(core_at != 0)
            def _():
                started(slab_copies(meta, odd[:4], odd[4:], u_ref, v_ref, first, 2), sems, 16 * first)

            return 0

        for e in range(SIDE):
            near = ((y + SIDE - e) % SIDE) * 2
            for src, k in ((rows[e], near + core_at), (rows[SIDE + e], near + 1 - core_at)):
                pltpu.make_async_copy(src.at[0], ru_ref.at[k], row_sems.at[k]).start()
                pltpu.make_async_copy(src.at[1], rv_ref.at[k], row_sems.at[panels + k]).start()
        lax.fori_loop(0, panels // 2, start_columns, 0)
        waited(four)

        def panel(step, _):
            k = ((y + SIDE - step // 2) % SIDE) * 2 + step % 2

            @pl.when(k % 2 == 0)
            def _():
                waits = slab_copies(meta, odd[:4], odd[4:], u_ref, v_ref, k, 2)
                waited([pltpu.make_async_copy(src, dst, sems.at[16 * k + i]) for i, (src, dst) in enumerate(waits)])

            pltpu.make_async_copy(rows[0].at[0], ru_ref.at[k], row_sems.at[k]).wait()
            pltpu.make_async_copy(rows[0].at[1], rv_ref.at[k], row_sems.at[panels + k]).wait()
            tile_panel(meta, k, tile_ref, u_ref, v_ref, ru_ref, rv_ref)
            rank = meta[4 + k]
            vk = v_ref[k]
            core = masked(tn(vk, vk), rank, rank)
            part = jnp.dot(u_ref[k, at, :], core, preferred_element_type=jnp.float32).astype(jnp.bfloat16)
            slab_ref[...] = slab_ref[...] - nt(part, u_ref[k])
            return 0

        lax.fori_loop(0, panels, panel, 0)
        waited(started([(tile_ref, out_hbm), (slab_ref, dout_hbm)], sems, 0))


def tile_scratch(panels, order, rank):
    stack = pltpu.VMEM((panels, order, rank), jnp.bfloat16)
    return [stack] * 4 + [pltpu.VMEM((order, order), jnp.float32), pltpu.VMEM((64, order), jnp.float32),
                          pltpu.SemaphoreType.DMA((130,)), pltpu.SemaphoreType.DMA((2 * panels,))]


def moved(value, pairs):
    return lax.ppermute(value, AXES, pairs)


def along(axis, change, parity):
    pairs = []
    for x in range(SIDE):
        for z in range(SIDE):
            for col in range(parity, 8, 2):
                to = (change(x), z) if axis == "x" else (x, change(z))
                pairs.append(((x * SIDE + z) * 8 + col, (to[0] * SIDE + to[1]) * 8 + col))
    return pairs


def across(change):
    return [(row * 8 + col, row * 8 + change(col)) for row in range(16) for col in range(8)]


def first_leg(a, b, parity):
    a, b = a[None], b[None]
    for change in (lambda p: p ^ 1, lambda p: p ^ 3):
        got_a = moved(a, along("x", change, parity))
        got_b = moved(b, along("z", change, parity))
        a, b = jnp.concatenate([a, got_a]), jnp.concatenate([b, got_b])
    return a, b


def second_leg(a, b, parity):
    got_a, got_b = [a, None, None, None], [b, None, None, None]
    for d in (1, 2, 3):
        got_a[d] = moved(a, along("z", lambda p: (p + d) % SIDE, parity))
        got_b[d] = moved(b, along("x", lambda p: (p + d) % SIDE, parity))
    return got_a, got_b


def shards(band, diag, row_factors, row_ranks, col_factors, col_ranks):
    column = lax.axis_index("cols")
    slab = lax.axis_index("rows")
    panels, slab_rows = col_factors.shape[0], diag.shape[1]
    order, rank = row_factors.shape[3], row_factors.shape[4]
    own_ranks = lax.dynamic_index_in_dim(col_ranks, column, 0, keepdims=False)
    meta = jnp.concatenate([jnp.stack([column, slab // SIDE, slab % SIDE, slab]).astype(jnp.int32), own_ranks])

    turned = row_factors[0, 0, 1].reshape(order // rank, rank, rank).transpose(0, 2, 1)
    kept = (jnp.arange(rank, dtype=jnp.int32) < row_ranks[0, 0])[None, :, None]
    turned = jnp.where(kept, turned, jnp.zeros((), turned.dtype)).reshape(order, rank)
    mine = jnp.stack([row_factors[0, 0, 0], turned])

    own = lax.all_to_all(col_factors, "cols", split_axis=0, concat_axis=1, tiled=True)[0]
    pieces = diag[0].reshape(slab_rows, 4, rank).transpose(1, 0, 2)
    rounded = lax.reduce_precision(pieces, exponent_bits=8, mantissa_bits=7)
    high = rounded.astype(jnp.bfloat16)
    low = (pieces - rounded).astype(jnp.bfloat16)
    own, mine, meta, high, low = lax.optimization_barrier((own, mine, meta, high, low))
    near = [mine]
    for d in (1, 2, 3):
        near.append(moved(mine, across(lambda c: ((c // 2 + d) % SIDE) * 2 + c % 2)))
    sides, bases = own[:, 1], own[:, 0]
    a, b = lax.optimization_barrier(first_leg(jnp.concatenate([sides, high]), jnp.concatenate([bases, low]), 0))
    fs, gs = second_leg(a, b, 0)
    far = [moved(p, across(lambda c: c ^ 1)) for p in near]
    odd_a, odd_b = lax.optimization_barrier(first_leg(sides, bases, 1))
    odd_fs, odd_gs = second_leg(odd_a, odd_b, 1)
    fs, gs, near, far, own_a, own_b = lax.optimization_barrier((fs, gs, near, far, odd_fs[0], odd_gs[0]))
    odd_fs, odd_gs = [own_a] + odd_fs[1:], [own_b] + odd_gs[1:]

    hbm = pl.BlockSpec(memory_space=pl.ANY)
    smem = pl.BlockSpec(memory_space=pltpu.SMEM)
    outs = (jax.ShapeDtypeStruct((order, order), jnp.float32), jax.ShapeDtypeStruct((slab_rows, order), jnp.float32))
    params = pltpu.CompilerParams(vmem_limit_bytes=COLUMN_GRANT)
    tile, slab_out = pl.pallas_call(
        column_kernel,
        out_shape=outs,
        in_specs=[smem] + [hbm] * 17,
        out_specs=(hbm, hbm),
        scratch_shapes=column_scratch(panels, order, rank),
        cost_estimate=pl.CostEstimate(flops=60_000_000_000, bytes_accessed=20_000_000, transcendentals=0),
        compiler_params=params, name="column")(meta, *fs, *gs, *near, *far, band[0, 0])

    tile, slab_out = pl.pallas_call(
        tile_kernel,
        out_shape=outs,
        in_specs=[smem] + [hbm] * 28,
        out_specs=(hbm, hbm),
        scratch_shapes=tile_scratch(panels, order, rank),
        input_output_aliases={27: 0, 28: 1},
        cost_estimate=pl.CostEstimate(flops=10_000_000_000, bytes_accessed=40_000_000, transcendentals=0),
        compiler_params=pltpu.CompilerParams(vmem_limit_bytes=TILE_GRANT), name="tile")(
            meta, *fs, *gs, *odd_fs, *odd_gs, *near, *far, band[0, 0], diag[0], tile, slab_out)
    return tile[None, None], slab_out[None]


def solution(mesh):
    placed = (
        P("rows", "cols", None, None),
        P("cols", "rows", None),
        P("rows", "cols", None, None, None),
        P("rows", "cols"),
        P(None, "cols", None, "rows", None),
        P(),
    )
    return jax.shard_map(
        shards,
        mesh=mesh,
        in_specs=placed,
        out_specs=(P("rows", "cols", None, None), P("cols", "rows", None)),
        check_vma=False,
    )
```

```python
import jax
import jax.numpy as jnp
from jax import lax
from jax.experimental import pallas as pl
from jax.experimental.pallas import tpu as pltpu
from jax.sharding import PartitionSpec as P


NB = 128
G = 8
SIDE = 4
AXES = ("rows", "cols")
NEAR = (0, 1, 3, 2)
COLUMN_GRANT = 46 << 20
TILE_GRANT = 60 << 20


def split2(x):
    hi = x.astype(jnp.bfloat16)
    lo = (x - hi.astype(jnp.float32)).astype(jnp.bfloat16)
    return hi, lo


def nt(a, b):
    return lax.dot_general(a, b, (((1,), (1,)), ((), ())), preferred_element_type=jnp.float32)


def nt3(ah, al, bh, bl):
    return nt(jnp.concatenate([ah, al, ah], axis=1), jnp.concatenate([bh, bh, bl], axis=1))


def lane_splat(x, lane):
    return jnp.broadcast_to(x[:, lane:lane + 1], x.shape)


def row_splat(x, s):
    return jnp.broadcast_to(x[s:s + 1, :], x.shape)


def factor_block(t_ref, up_ref, one_ref):
    one = one_ref[...]
    sub = lax.broadcasted_iota(jnp.int32, (G, NB), 0)
    lane = lax.broadcasted_iota(jnp.int32, (G, NB), 1)
    count = NB // G
    first = t_ref[0:G, :]
    diag = [lane_splat(first, c) * one for c in range(G)]
    for g in range(count):
        base = g * G
        v = t_ref[base:base + G, :]
        b = [[row_splat(diag[j], s) if s >= j else None for j in range(G)] for s in range(G)]
        more = g + 1 < count
        if more:
            below = t_ref[base + G:base + 2 * G, :]
            wn = [lane_splat(below, base + j) for j in range(G)]
            diag = [lane_splat(below, base + G + c) for c in range(G)]
        inside = (lane >= base) & (lane < base + G)
        vi = jnp.where(inside, jnp.where(lane - base == sub, 1.0, 0.0), v)
        low = [[None] * G for _ in range(G)]
        rinv = [None] * G
        ra = [row_splat(v, s) for s in range(G)]
        r = [row_splat(vi, s) for s in range(G)]
        for j in range(G):
            rinv[j] = lax.rsqrt(b[j][j])
            for s in range(j + 1, G):
                low[s][j] = b[s][j] * rinv[j]
            for t in range(j + 1, G):
                for s in range(t, G):
                    b[s][t] = b[s][t] - low[s][j] * low[t][j]
            if more:
                ln = wn[j] * rinv[j]
                for t in range(j + 1, G):
                    wn[t] = wn[t] - ln * low[t][j]
                for c in range(G):
                    diag[c] = diag[c] - ln * row_splat(ln, c)
            ra[j] = ra[j] * rinv[j]
            r[j] = r[j] * rinv[j]
            for s in range(j + 1, G):
                ra[s] = ra[s] - low[s][j] * ra[j]
                r[s] = r[s] - low[s][j] * r[j]
        out, outa = r[0], ra[0]
        for s in range(1, G):
            out = jnp.where(sub == s, r[s], out)
            outa = jnp.where(sub == s, ra[s], outa)
        up_ref[base:base + G, :] = outa
        t_ref[base:base + G, :] = out
        if more:
            m = [None] * G
            for s in reversed(range(G)):
                acc = r[s]
                for t in range(s + 1, G):
                    acc = acc - low[t][s] * m[t]
                m[s] = acc * rinv[s]
            for rb in range(g + 1, count):
                w = t_ref[rb * G:(rb + 1) * G, :]
                acc = jnp.where(inside, 0.0, w)
                for j in range(G):
                    acc = acc - lane_splat(w, base + j) * m[j]
                t_ref[rb * G:(rb + 1) * G, :] = acc


def chol_body(a_ref, inv_ref, t_ref, up_ref, one_ref, beside):
    n = a_ref.shape[0]
    nblk = n // NB
    ri = lax.broadcasted_iota(jnp.int32, (NB, NB), 0)
    ci = lax.broadcasted_iota(jnp.int32, (NB, NB), 1)

    def step(j, _):
        o = pl.multiple_of(j * NB, NB)
        t_ref[...] = a_ref[pl.ds(o, NB), pl.ds(o, NB)]
        factor_block(t_ref, up_ref, one_ref)
        beside(j)
        inv = jnp.where(ri >= ci, t_ref[...], 0.0)
        inv_ref[pl.ds(o, NB), :] = inv
        low = jnp.where(ri >= ci, up_ref[...].T, 0.0)
        ih, il = split2(inv)
        for v in range(nblk // 2):
            lo_row = 2 * NB * v

            @pl.when((j + 1) // 2 == v)
            def _():
                p = a_ref[lo_row:, pl.ds(o, NB)]
                ph, plo = split2(p)
                x = nt3(ph, plo, ih, il)
                rows = lax.broadcasted_iota(jnp.int32, x.shape, 0) + lo_row
                x = jnp.where(rows >= o + NB, x, 0.0)
                a_ref[lo_row:, pl.ds(o, NB)] = x
                xh, xl = split2(x)
                c = nt3(xh, xl, xh, xl)
                a_ref[lo_row:, lo_row:] = a_ref[lo_row:, lo_row:] - c
        a_ref[pl.ds(o, NB), pl.ds(o, NB)] = low
        return 0

    lax.fori_loop(0, nblk, step, 0)


def solve_body(b_ref, l_ref, inv_ref, x_ref, xh_ref, xl_ref, done):
    n = b_ref.shape[0]
    for j in range(n // (2 * NB)):
        o = 2 * NB * j
        s = slice(o, o + 2 * NB)
        i0, i1 = inv_ref[o:o + NB, :], inv_ref[o + NB:o + 2 * NB, :]
        i0h, i0l = split2(i0.T)
        i1h, i1l = split2(i1)
        mh, ml = split2(nt3(*split2(l_ref[o + NB:o + 2 * NB, o:o + NB]), i0h, i0l))
        off = -nt3(i1h, i1l, *split2(nt_same(mh, ml)))
        inv = jnp.concatenate([jnp.concatenate([i0, jnp.zeros_like(i0)], axis=1), jnp.concatenate([off, i1], axis=1)], axis=0)
        ih, il = split2(inv)
        acc = b_ref[:, s]
        if j:
            lh, ll = split2(l_ref[s, :o])
            acc = acc - nt(xh_ref[:, :o], lh) - nt(xl_ref[:, :o], lh) - nt(xh_ref[:, :o], ll)
        ah, al = split2(acc)
        x = nt3(ah, al, ih, il)
        x_ref[:, s] = x
        done(j, s)
        xh, xl = split2(x)
        xh_ref[:, s] = xh
        xl_ref[:, s] = xl


def nt_same(mh, ml):
    return (mh.astype(jnp.float32) + ml.astype(jnp.float32)).T


def tn(a, b):
    return lax.dot_general(a, b, (((0,), (0,)), ((), ())), preferred_element_type=jnp.float32)


def masked(core, rank_a, rank_b):
    kept = lax.broadcasted_iota(jnp.int32, core.shape, 1) < rank_b
    if rank_a is not None:
        kept = kept & (lax.broadcasted_iota(jnp.int32, core.shape, 0) < rank_a)
    return jnp.where(kept, core, 0.0).astype(jnp.bfloat16)


def started(pairs, sems, first=0):
    copies = [pltpu.make_async_copy(src, dst, sems.at[first + n]) for n, (src, dst) in enumerate(pairs)]
    for copy in copies:
        copy.start()
    return copies


def waited(copies):
    for copy in copies:
        copy.wait()


def slab_copies(meta, fs, gs, u_ref, v_ref, first, count, to=None):
    x, z = meta[1], meta[2]
    pairs = []
    for e in range(SIDE):
        for d in range(SIDE):
            for far, near, at_x, at_z, dst in (
                (e, d, x ^ NEAR[d], (z + SIDE - e) % SIDE, v_ref), (d, e, (x + SIDE - d) % SIDE, z ^ NEAR[e], u_ref)
            ):
                at = pl.ds(pl.multiple_of((at_x * SIDE + at_z) * 64, 64), 64)
                stacks = fs if dst is v_ref else gs
                if len(stacks) == SIDE:
                    src, near = stacks[far], near
                elif far == 2:
                    src, near = stacks[2 + near // 2], near % 2
                else:
                    src = stacks[(0, 1, None, 4)[far]]
                pairs.append((src.at[near, pl.ds(first, count)], dst.at[pl.ds(first if to is None else to, count), at, :]))
    return pairs


def row_copies(meta, rows, ru_ref, rv_ref):
    y, core_at = meta[0] // 2, meta[0] % 2
    pairs = []
    for e in range(SIDE):
        near = ((y + SIDE - e) % SIDE) * 2
        for src, k in ((rows[e], near + core_at), (rows[SIDE + e], near + 1 - core_at)):
            pairs.append((src.at[0], ru_ref.at[k]))
            pairs.append((src.at[1], rv_ref.at[k]))
    return pairs


def tile_panel(meta, k, tile_ref, u_ref, v_ref, ru_ref, rv_ref):
    n = tile_ref.shape[0]
    core = jnp.dot(rv_ref[k, 0:256], v_ref[k, 0:256], preferred_element_type=jnp.float32)
    for q in range(256, n, 256):
        core = core + jnp.dot(rv_ref[k, q:q + 256], v_ref[k, q:q + 256], preferred_element_type=jnp.float32)
    core = masked(core, None, meta[4 + k])
    left = jnp.dot(ru_ref[k], core, preferred_element_type=jnp.float32).astype(jnp.bfloat16)
    uk = u_ref[k]
    for s in range(0, n, 512):
        tile_ref[s:s + 512, :] = tile_ref[s:s + 512, :] - nt(left[s:s + 512], uk)


def column_kernel(meta, *refs):
    fs, gs, rows = refs[0:5], refs[5:10], refs[10:18]
    band_hbm, out_hbm, dout_hbm = refs[18:21]
    (u_ref, v_ref, hi_ref, lo_ref, ru_ref, rv_ref, tile_ref, acc_ref, l_ref, inv_ref, t_ref, up_ref, one_ref, xh_ref, xl_ref, sems) = refs[21:]
    n = l_ref.shape[0]

    @pl.when(meta[0] == 0)
    def _():
        one = started(slab_copies(meta, fs, gs, u_ref, v_ref, 0, 4), sems, 0)
        two = started(slab_copies(meta, fs, gs, u_ref, v_ref, 4, 4), sems, 32)
        three = started(slab_copies(meta, fs, gs, lo_ref, hi_ref, 8, 4, 0), sems, 64)
        acc_ref[...] = jnp.zeros_like(acc_ref)

        four = [pltpu.make_async_copy(src, dst, sems.at[96 + n])
                for n, (src, dst) in enumerate(row_copies(meta, rows, ru_ref, rv_ref) + [(band_hbm, tile_ref)])]

        def panel(k, _):
            @pl.when(k == 4)
            def _():
                waited(two)
                for copy in four:
                    copy.start()

            rank = meta[4 + k]
            vk, uk = v_ref[k], u_ref[k]
            core = masked(tn(vk, vk), rank, rank)
            left = jnp.dot(uk, core, preferred_element_type=jnp.float32).astype(jnp.bfloat16)
            for s in range(0, n, 512):
                acc_ref[s:s + 512, :] = acc_ref[s:s + 512, :] - nt(left[s:s + 512], uk)
            return 0

        waited(one)
        lax.fori_loop(0, 8, panel, 0)
        waited(three)

        def whole(rows, cols):
            q, at = cols.start // 256, slice(cols.start % 256, cols.start % 256 + NB)
            return acc_ref[rows, cols] + (hi_ref[q, rows, at].astype(jnp.float32) + lo_ref[q, rows, at].astype(jnp.float32))

        for i in range(n // NB):
            si = slice(i * NB, (i + 1) * NB)
            for j in range(i + 1):
                sj = slice(j * NB, (j + 1) * NB)
                l_ref[si, sj] = (whole(si, sj) + whole(sj, si).T) * 0.5
        waited(four)
        one_ref[...] = jnp.ones_like(one_ref)
        chol_body(l_ref, inv_ref, t_ref, up_ref, one_ref, lambda j: tile_panel(meta, j, tile_ref, u_ref, v_ref, ru_ref, rv_ref))
        for j in range(n // NB - 1):
            l_ref[j * NB:(j + 1) * NB, (j + 1) * NB:] = jnp.zeros((NB, n - (j + 1) * NB), jnp.float32)
        last = started([(l_ref.at[pl.ds(pl.multiple_of(meta[3] * 64, 64), 64), :], dout_hbm)], sems, 0)

        def done(j, s):
            last.extend(started([(tile_ref.at[:, s], out_hbm.at[:, s])], sems, 1 + j))

        solve_body(tile_ref, l_ref, inv_ref, tile_ref, xh_ref, xl_ref, done)
        waited(last)


def column_scratch(panels, order, rank):
    stack = pltpu.VMEM((panels, order, rank), jnp.bfloat16)
    quarter = pltpu.VMEM((4, order, rank), jnp.bfloat16)
    square = pltpu.VMEM((order, order), jnp.float32)
    block = pltpu.VMEM((NB, NB), jnp.float32)
    return [stack, stack, quarter, quarter, stack, stack, square, square, square,
            pltpu.VMEM((order, NB), jnp.float32), block, block, pltpu.VMEM((G, NB), jnp.float32),
            pltpu.VMEM((order, order), jnp.bfloat16), pltpu.VMEM((order, order), jnp.bfloat16),
            pltpu.SemaphoreType.DMA((128,))]


def tile_kernel(meta, *refs):
    even, odd, rows = refs[0:10], refs[10:18], refs[18:26]
    band_hbm, diag_hbm, _, _, out_hbm, dout_hbm = refs[26:32]
    u_ref, v_ref, ru_ref, rv_ref, tile_ref, slab_ref, sems, row_sems = refs[32:]
    panels = u_ref.shape[0]
    at = pl.ds(pl.multiple_of(meta[3] * 64, 64), 64)
    y, core_at = meta[0] // 2, meta[0] % 2

    @pl.when(meta[0] != 0)
    def _():
        four = started([(band_hbm, tile_ref), (diag_hbm, slab_ref)], sems, 128)

        def start_columns(group, _):
            first = ((y + SIDE - group) % SIDE) * 2

            @pl.when(core_at == 0)
            def _():
                started(slab_copies(meta, even[:5], even[5:], u_ref, v_ref, first, 2), sems, 16 * first)

            @pl.when(core_at != 0)
            def _():
                started(slab_copies(meta, odd[:4], odd[4:], u_ref, v_ref, first, 2), sems, 16 * first)

            return 0

        for e in range(SIDE):
            near = ((y + SIDE - e) % SIDE) * 2
            for src, k in ((rows[e], near + core_at), (rows[SIDE + e], near + 1 - core_at)):
                pltpu.make_async_copy(src.at[0], ru_ref.at[k], row_sems.at[k]).start()
                pltpu.make_async_copy(src.at[1], rv_ref.at[k], row_sems.at[panels + k]).start()
        lax.fori_loop(0, panels // 2, start_columns, 0)
        waited(four)

        def panel(step, _):
            k = ((y + SIDE - step // 2) % SIDE) * 2 + step % 2

            @pl.when(k % 2 == 0)
            def _():
                waits = slab_copies(meta, odd[:4], odd[4:], u_ref, v_ref, k, 2)
                waited([pltpu.make_async_copy(src, dst, sems.at[16 * k + i]) for i, (src, dst) in enumerate(waits)])

            pltpu.make_async_copy(rows[0].at[0], ru_ref.at[k], row_sems.at[k]).wait()
            pltpu.make_async_copy(rows[0].at[1], rv_ref.at[k], row_sems.at[panels + k]).wait()
            tile_panel(meta, k, tile_ref, u_ref, v_ref, ru_ref, rv_ref)
            rank = meta[4 + k]
            vk = v_ref[k]
            core = masked(tn(vk, vk), rank, rank)
            part = jnp.dot(u_ref[k, at, :], core, preferred_element_type=jnp.float32).astype(jnp.bfloat16)
            slab_ref[...] = slab_ref[...] - nt(part, u_ref[k])
            return 0

        lax.fori_loop(0, panels, panel, 0)
        waited(started([(tile_ref, out_hbm), (slab_ref, dout_hbm)], sems, 0))


def tile_scratch(panels, order, rank):
    stack = pltpu.VMEM((panels, order, rank), jnp.bfloat16)
    return [stack] * 4 + [pltpu.VMEM((order, order), jnp.float32), pltpu.VMEM((64, order), jnp.float32),
                          pltpu.SemaphoreType.DMA((130,)), pltpu.SemaphoreType.DMA((2 * panels,))]


def moved(value, pairs):
    return lax.ppermute(value, AXES, pairs)


def along(axis, change, parity):
    pairs = []
    for x in range(SIDE):
        for z in range(SIDE):
            for col in range(parity, 8, 2):
                to = (change(x), z) if axis == "x" else (x, change(z))
                pairs.append(((x * SIDE + z) * 8 + col, (to[0] * SIDE + to[1]) * 8 + col))
    return pairs


def across(change):
    return [(row * 8 + col, row * 8 + change(col)) for row in range(16) for col in range(8)]


def first_leg(a, b, parity):
    a, b = a[None], b[None]
    for change in (lambda p: p ^ 1, lambda p: p ^ 3):
        got_a = moved(a, along("x", change, parity))
        got_b = moved(b, along("z", change, parity))
        a, b = jnp.concatenate([a, got_a]), jnp.concatenate([b, got_b])
    return a, b


def second_leg(a, b, parity):
    got_a, got_b = [a, None, None, None], [b, None, None, None]
    for d in (1, 2, 3):
        got_a[d] = moved(a, along("z", lambda p: (p + d) % SIDE, parity))
        got_b[d] = moved(b, along("x", lambda p: (p + d) % SIDE, parity))
    return got_a, got_b


def ring_leg(a, b):
    ahead, back = (lambda p: (p + 1) % SIDE), (lambda p: (p + 3) % SIDE)
    got = {}
    for step, change in ((1, ahead), (3, back)):
        for side, value, axis in (("a", a, "z"), ("b", b, "x")):
            got[side, step] = moved(value, along(axis, change, 0))
    half = a.shape[0] // 2
    for step, change, part in ((1, ahead, slice(0, half)), (3, back, slice(half, 2 * half))):
        for side, axis in (("a", "z"), ("b", "x")):
            got[side, 2, step] = moved(got[side, step][part], along(axis, change, 0))
    return [[own, got[side, 1], got[side, 2, 1], got[side, 2, 3], got[side, 3]] for side, own in (("a", a), ("b", b))]


def shards(band, diag, row_factors, row_ranks, col_factors, col_ranks):
    column = lax.axis_index("cols")
    slab = lax.axis_index("rows")
    panels, slab_rows = col_factors.shape[0], diag.shape[1]
    order, rank = row_factors.shape[3], row_factors.shape[4]
    own_ranks = lax.dynamic_index_in_dim(col_ranks, column, 0, keepdims=False)
    meta = jnp.concatenate([jnp.stack([column, slab // SIDE, slab % SIDE, slab]).astype(jnp.int32), own_ranks])

    turned = row_factors[0, 0, 1].reshape(order // rank, rank, rank).transpose(0, 2, 1)
    kept = (jnp.arange(rank, dtype=jnp.int32) < row_ranks[0, 0])[None, :, None]
    turned = jnp.where(kept, turned, jnp.zeros((), turned.dtype)).reshape(order, rank)
    mine = jnp.stack([row_factors[0, 0, 0], turned])

    own = lax.all_to_all(col_factors, "cols", split_axis=0, concat_axis=1, tiled=True)[0]
    pieces = diag[0].reshape(slab_rows, 4, rank).transpose(1, 0, 2)
    rounded = lax.reduce_precision(pieces, exponent_bits=8, mantissa_bits=7)
    high = rounded.astype(jnp.bfloat16)
    low = (pieces - rounded).astype(jnp.bfloat16)
    own, mine, meta, high, low = lax.optimization_barrier((own, mine, meta, high, low))
    near = [mine]
    for d in (1, 2, 3):
        near.append(moved(mine, across(lambda c: ((c // 2 + d) % SIDE) * 2 + c % 2)))
    sides, bases = own[:, 1], own[:, 0]
    a, b = lax.optimization_barrier(first_leg(jnp.concatenate([sides, high]), jnp.concatenate([bases, low]), 0))
    fs, gs = ring_leg(a, b)
    far = [moved(p, across(lambda c: c ^ 1)) for p in near]
    odd_a, odd_b = lax.optimization_barrier(first_leg(sides, bases, 1))
    odd_fs, odd_gs = second_leg(odd_a, odd_b, 1)
    fs, gs, near, far, own_a, own_b = lax.optimization_barrier((fs, gs, near, far, odd_fs[0], odd_gs[0]))
    odd_fs, odd_gs = [own_a] + odd_fs[1:], [own_b] + odd_gs[1:]

    hbm = pl.BlockSpec(memory_space=pl.ANY)
    smem = pl.BlockSpec(memory_space=pltpu.SMEM)
    outs = (jax.ShapeDtypeStruct((order, order), jnp.float32), jax.ShapeDtypeStruct((slab_rows, order), jnp.float32))
    params = pltpu.CompilerParams(vmem_limit_bytes=COLUMN_GRANT)
    tile, slab_out = pl.pallas_call(
        column_kernel,
        out_shape=outs,
        in_specs=[smem] + [hbm] * 19,
        out_specs=(hbm, hbm),
        scratch_shapes=column_scratch(panels, order, rank),
        cost_estimate=pl.CostEstimate(flops=60_000_000_000, bytes_accessed=20_000_000, transcendentals=0),
        compiler_params=params, name="column")(meta, *fs, *gs, *near, *far, band[0, 0])

    tile, slab_out = pl.pallas_call(
        tile_kernel,
        out_shape=outs,
        in_specs=[smem] + [hbm] * 30,
        out_specs=(hbm, hbm),
        scratch_shapes=tile_scratch(panels, order, rank),
        input_output_aliases={29: 0, 30: 1},
        cost_estimate=pl.CostEstimate(flops=10_000_000_000, bytes_accessed=40_000_000, transcendentals=0),
        compiler_params=pltpu.CompilerParams(vmem_limit_bytes=TILE_GRANT), name="tile")(
            meta, *fs, *gs, *odd_fs, *odd_gs, *near, *far, band[0, 0], diag[0], tile, slab_out)
    return tile[None, None], slab_out[None]


def solution(mesh):
    placed = (
        P("rows", "cols", None, None),
        P("cols", "rows", None),
        P("rows", "cols", None, None, None),
        P("rows", "cols"),
        P(None, "cols", None, "rows", None),
        P(),
    )
    return jax.shard_map(
        shards,
        mesh=mesh,
        in_specs=placed,
        out_specs=(P("rows", "cols", None, None), P("cols", "rows", None)),
        check_vma=False,
    )
```

```python
import jax
import jax.numpy as jnp
from jax import lax
from jax.experimental import pallas as pl
from jax.experimental.pallas import tpu as pltpu
from jax.sharding import PartitionSpec as P


NB = 128
G = 8
SIDE = 4
AXES = ("rows", "cols")
NEAR = (0, 1, 3, 2)
COLUMN_GRANT = 46 << 20
TILE_GRANT = 60 << 20


def split2(x):
    hi = x.astype(jnp.bfloat16)
    lo = (x - hi.astype(jnp.float32)).astype(jnp.bfloat16)
    return hi, lo


def nt(a, b):
    return lax.dot_general(a, b, (((1,), (1,)), ((), ())), preferred_element_type=jnp.float32)


def nt3(ah, al, bh, bl):
    return nt(jnp.concatenate([ah, al, ah], axis=1), jnp.concatenate([bh, bh, bl], axis=1))


def lane_splat(x, lane):
    return jnp.broadcast_to(x[:, lane:lane + 1], x.shape)


def row_splat(x, s):
    return jnp.broadcast_to(x[s:s + 1, :], x.shape)


def factor_block(t_ref, up_ref, one_ref):
    one = one_ref[...]
    sub = lax.broadcasted_iota(jnp.int32, (G, NB), 0)
    lane = lax.broadcasted_iota(jnp.int32, (G, NB), 1)
    count = NB // G
    first = t_ref[0:G, :]
    diag = [lane_splat(first, c) * one for c in range(G)]
    for g in range(count):
        base = g * G
        v = t_ref[base:base + G, :]
        b = [[row_splat(diag[j], s) if s >= j else None for j in range(G)] for s in range(G)]
        more = g + 1 < count
        if more:
            below = t_ref[base + G:base + 2 * G, :]
            wn = [lane_splat(below, base + j) for j in range(G)]
            diag = [lane_splat(below, base + G + c) for c in range(G)]
        inside = (lane >= base) & (lane < base + G)
        vi = jnp.where(inside, jnp.where(lane - base == sub, 1.0, 0.0), v)
        low = [[None] * G for _ in range(G)]
        rinv = [None] * G
        ra = [row_splat(v, s) for s in range(G)]
        r = [row_splat(vi, s) for s in range(G)]
        for j in range(G):
            rinv[j] = lax.rsqrt(b[j][j])
            for s in range(j + 1, G):
                low[s][j] = b[s][j] * rinv[j]
            for t in range(j + 1, G):
                for s in range(t, G):
                    b[s][t] = b[s][t] - low[s][j] * low[t][j]
            if more:
                ln = wn[j] * rinv[j]
                for t in range(j + 1, G):
                    wn[t] = wn[t] - ln * low[t][j]
                for c in range(G):
                    diag[c] = diag[c] - ln * row_splat(ln, c)
            ra[j] = ra[j] * rinv[j]
            r[j] = r[j] * rinv[j]
            for s in range(j + 1, G):
                ra[s] = ra[s] - low[s][j] * ra[j]
                r[s] = r[s] - low[s][j] * r[j]
        out, outa = r[0], ra[0]
        for s in range(1, G):
            out = jnp.where(sub == s, r[s], out)
            outa = jnp.where(sub == s, ra[s], outa)
        up_ref[base:base + G, :] = outa
        t_ref[base:base + G, :] = out
        if more:
            m = [None] * G
            for s in reversed(range(G)):
                acc = r[s]
                for t in range(s + 1, G):
                    acc = acc - low[t][s] * m[t]
                m[s] = acc * rinv[s]
            for rb in range(g + 1, count):
                w = t_ref[rb * G:(rb + 1) * G, :]
                acc = jnp.where(inside, 0.0, w)
                for j in range(G):
                    acc = acc - lane_splat(w, base + j) * m[j]
                t_ref[rb * G:(rb + 1) * G, :] = acc


def chol_body(a_ref, inv_ref, t_ref, up_ref, one_ref, beside):
    n = a_ref.shape[0]
    nblk = n // NB
    ri = lax.broadcasted_iota(jnp.int32, (NB, NB), 0)
    ci = lax.broadcasted_iota(jnp.int32, (NB, NB), 1)

    def step(j, _):
        o = pl.multiple_of(j * NB, NB)
        t_ref[...] = a_ref[pl.ds(o, NB), pl.ds(o, NB)]
        factor_block(t_ref, up_ref, one_ref)
        beside(j)
        inv = jnp.where(ri >= ci, t_ref[...], 0.0)
        inv_ref[pl.ds(o, NB), :] = inv
        low = jnp.where(ri >= ci, up_ref[...].T, 0.0)
        ih, il = split2(inv)
        for v in range(nblk // 2):
            lo_row = 2 * NB * v

            @pl.when((j + 1) // 2 == v)
            def _():
                p = a_ref[lo_row:, pl.ds(o, NB)]
                ph, plo = split2(p)
                x = nt3(ph, plo, ih, il)
                rows = lax.broadcasted_iota(jnp.int32, x.shape, 0) + lo_row
                x = jnp.where(rows >= o + NB, x, 0.0)
                a_ref[lo_row:, pl.ds(o, NB)] = x
                xh, xl = split2(x)
                c = nt3(xh, xl, xh, xl)
                a_ref[lo_row:, lo_row:] = a_ref[lo_row:, lo_row:] - c
        a_ref[pl.ds(o, NB), pl.ds(o, NB)] = low
        return 0

    lax.fori_loop(0, nblk, step, 0)


def solve_body(b_ref, l_ref, inv_ref, x_ref, xh_ref, xl_ref, done):
    n = b_ref.shape[0]
    for j in range(n // (2 * NB)):
        o = 2 * NB * j
        s = slice(o, o + 2 * NB)
        i0, i1 = inv_ref[o:o + NB, :], inv_ref[o + NB:o + 2 * NB, :]
        i0h, i0l = split2(i0.T)
        i1h, i1l = split2(i1)
        mh, ml = split2(nt3(*split2(l_ref[o + NB:o + 2 * NB, o:o + NB]), i0h, i0l))
        off = -nt3(i1h, i1l, *split2(nt_same(mh, ml)))
        inv = jnp.concatenate([jnp.concatenate([i0, jnp.zeros_like(i0)], axis=1), jnp.concatenate([off, i1], axis=1)], axis=0)
        ih, il = split2(inv)
        acc = b_ref[:, s]
        if j:
            lh, ll = split2(l_ref[s, :o])
            acc = acc - nt(xh_ref[:, :o], lh) - nt(xl_ref[:, :o], lh) - nt(xh_ref[:, :o], ll)
        ah, al = split2(acc)
        x = nt3(ah, al, ih, il)
        x_ref[:, s] = x
        done(j, s)
        xh, xl = split2(x)
        xh_ref[:, s] = xh
        xl_ref[:, s] = xl


def nt_same(mh, ml):
    return (mh.astype(jnp.float32) + ml.astype(jnp.float32)).T


def tn(a, b):
    return lax.dot_general(a, b, (((0,), (0,)), ((), ())), preferred_element_type=jnp.float32)


def masked(core, rank_a, rank_b):
    kept = lax.broadcasted_iota(jnp.int32, core.shape, 1) < rank_b
    if rank_a is not None:
        kept = kept & (lax.broadcasted_iota(jnp.int32, core.shape, 0) < rank_a)
    return jnp.where(kept, core, 0.0).astype(jnp.bfloat16)


def started(pairs, sems, first=0):
    copies = [pltpu.make_async_copy(src, dst, sems.at[first + n]) for n, (src, dst) in enumerate(pairs)]
    for copy in copies:
        copy.start()
    return copies


def waited(copies):
    for copy in copies:
        copy.wait()


def slab_copies(meta, fs, gs, u_ref, v_ref, first, count, to=None):
    x, z = meta[1], meta[2]
    pairs = []
    for e in range(SIDE):
        for d in range(SIDE):
            for far, near, at_x, at_z, dst in (
                (e, d, x ^ NEAR[d], (z + SIDE - e) % SIDE, v_ref), (d, e, (x + SIDE - d) % SIDE, z ^ NEAR[e], u_ref)
            ):
                at = pl.ds(pl.multiple_of((at_x * SIDE + at_z) * 64, 64), 64)
                src = fs[far] if dst is v_ref else gs[far]
                pairs.append((src.at[near, pl.ds(first, count)], dst.at[pl.ds(first if to is None else to, count), at, :]))
    return pairs


def row_copies(meta, rows, ru_ref, rv_ref):
    y, core_at = meta[0] // 2, meta[0] % 2
    pairs = []
    for e in range(SIDE):
        near = ((y + SIDE - e) % SIDE) * 2
        for src, k in ((rows[e], near + core_at), (rows[SIDE + e], near + 1 - core_at)):
            pairs.append((src.at[0], ru_ref.at[k]))
            pairs.append((src.at[1], rv_ref.at[k]))
    return pairs


def tile_panel(meta, k, tile_ref, u_ref, v_ref, ru_ref, rv_ref):
    n = tile_ref.shape[0]
    core = jnp.dot(rv_ref[k, 0:256], v_ref[k, 0:256], preferred_element_type=jnp.float32)
    for q in range(256, n, 256):
        core = core + jnp.dot(rv_ref[k, q:q + 256], v_ref[k, q:q + 256], preferred_element_type=jnp.float32)
    core = masked(core, None, meta[4 + k])
    left = jnp.dot(ru_ref[k], core, preferred_element_type=jnp.float32).astype(jnp.bfloat16)
    uk = u_ref[k]
    for s in range(0, n, 512):
        tile_ref[s:s + 512, :] = tile_ref[s:s + 512, :] - nt(left[s:s + 512], uk)


def column_kernel(meta, *refs):
    fs, gs, rows = refs[0:4], refs[4:8], refs[8:16]
    band_hbm, out_hbm, dout_hbm = refs[16:19]
    (u_ref, v_ref, hi_ref, lo_ref, ru_ref, rv_ref, tile_ref, acc_ref, l_ref, inv_ref, t_ref, up_ref, one_ref, xh_ref, xl_ref, sems) = refs[19:]
    n = l_ref.shape[0]

    @pl.when(meta[0] == 0)
    def _():
        one = started(slab_copies(meta, fs, gs, u_ref, v_ref, 0, 4), sems, 0)
        two = started(slab_copies(meta, fs, gs, u_ref, v_ref, 4, 4), sems, 32)
        three = started(slab_copies(meta, fs, gs, lo_ref, hi_ref, 8, 4, 0), sems, 64)
        acc_ref[...] = jnp.zeros_like(acc_ref)

        four = [pltpu.make_async_copy(src, dst, sems.at[96 + n])
                for n, (src, dst) in enumerate(row_copies(meta, rows, ru_ref, rv_ref) + [(band_hbm, tile_ref)])]

        def panel(k, _):
            @pl.when(k == 4)
            def _():
                waited(two)
                for copy in four:
                    copy.start()

            rank = meta[4 + k]
            vk, uk = v_ref[k], u_ref[k]
            core = masked(tn(vk, vk), rank, rank)
            left = jnp.dot(uk, core, preferred_element_type=jnp.float32).astype(jnp.bfloat16)
            for s in range(0, n, 512):
                acc_ref[s:s + 512, :] = acc_ref[s:s + 512, :] - nt(left[s:s + 512], uk)
            return 0

        waited(one)
        lax.fori_loop(0, 8, panel, 0)
        waited(three)

        def whole(rows, cols):
            q, at = cols.start // 256, slice(cols.start % 256, cols.start % 256 + NB)
            return acc_ref[rows, cols] + (hi_ref[q, rows, at].astype(jnp.float32) + lo_ref[q, rows, at].astype(jnp.float32))

        for i in range(n // NB):
            si = slice(i * NB, (i + 1) * NB)
            for j in range(i + 1):
                sj = slice(j * NB, (j + 1) * NB)
                l_ref[si, sj] = (whole(si, sj) + whole(sj, si).T) * 0.5
        waited(four)
        one_ref[...] = jnp.ones_like(one_ref)
        chol_body(l_ref, inv_ref, t_ref, up_ref, one_ref, lambda j: tile_panel(meta, j, tile_ref, u_ref, v_ref, ru_ref, rv_ref))
        for j in range(n // NB - 1):
            l_ref[j * NB:(j + 1) * NB, (j + 1) * NB:] = jnp.zeros((NB, n - (j + 1) * NB), jnp.float32)
        last = started([(l_ref.at[pl.ds(pl.multiple_of(meta[3] * 64, 64), 64), :], dout_hbm)], sems, 0)

        def done(j, s):
            last.extend(started([(tile_ref.at[:, s], out_hbm.at[:, s])], sems, 1 + j))

        solve_body(tile_ref, l_ref, inv_ref, tile_ref, xh_ref, xl_ref, done)
        waited(last)


def column_scratch(panels, order, rank):
    stack = pltpu.VMEM((panels, order, rank), jnp.bfloat16)
    quarter = pltpu.VMEM((4, order, rank), jnp.bfloat16)
    square = pltpu.VMEM((order, order), jnp.float32)
    block = pltpu.VMEM((NB, NB), jnp.float32)
    return [stack, stack, quarter, quarter, stack, stack, square, square, square,
            pltpu.VMEM((order, NB), jnp.float32), block, block, pltpu.VMEM((G, NB), jnp.float32),
            pltpu.VMEM((order, order), jnp.bfloat16), pltpu.VMEM((order, order), jnp.bfloat16),
            pltpu.SemaphoreType.DMA((128,))]


def tile_kernel(meta, *refs):
    even, odd, rows = refs[0:8], refs[8:16], refs[16:24]
    band_hbm, diag_hbm, _, _, out_hbm, dout_hbm = refs[24:30]
    u_ref, v_ref, ru_ref, rv_ref, tile_ref, slab_ref, sems, row_sems = refs[30:]
    panels = u_ref.shape[0]
    at = pl.ds(pl.multiple_of(meta[3] * 64, 64), 64)
    y, core_at = meta[0] // 2, meta[0] % 2

    @pl.when(meta[0] != 0)
    def _():
        four = started([(band_hbm, tile_ref), (diag_hbm, slab_ref)], sems, 128)

        def start_columns(group, _):
            first = ((y + SIDE - group) % SIDE) * 2

            @pl.when(core_at == 0)
            def _():
                started(slab_copies(meta, even[:4], even[4:], u_ref, v_ref, first, 2), sems, 16 * first)

            @pl.when(core_at != 0)
            def _():
                started(slab_copies(meta, odd[:4], odd[4:], u_ref, v_ref, first, 2), sems, 16 * first)

            return 0

        for e in range(SIDE):
            near = ((y + SIDE - e) % SIDE) * 2
            for src, k in ((rows[e], near + core_at), (rows[SIDE + e], near + 1 - core_at)):
                pltpu.make_async_copy(src.at[0], ru_ref.at[k], row_sems.at[k]).start()
                pltpu.make_async_copy(src.at[1], rv_ref.at[k], row_sems.at[panels + k]).start()
        lax.fori_loop(0, panels // 2, start_columns, 0)
        waited(four)

        def panel(step, _):
            k = ((y + SIDE - step // 2) % SIDE) * 2 + step % 2

            @pl.when(k % 2 == 0)
            def _():
                waits = slab_copies(meta, odd[:4], odd[4:], u_ref, v_ref, k, 2)
                waited([pltpu.make_async_copy(src, dst, sems.at[16 * k + i]) for i, (src, dst) in enumerate(waits)])

            pltpu.make_async_copy(rows[0].at[0], ru_ref.at[k], row_sems.at[k]).wait()
            pltpu.make_async_copy(rows[0].at[1], rv_ref.at[k], row_sems.at[panels + k]).wait()
            tile_panel(meta, k, tile_ref, u_ref, v_ref, ru_ref, rv_ref)
            rank = meta[4 + k]
            vk = v_ref[k]
            core = masked(tn(vk, vk), rank, rank)
            part = jnp.dot(u_ref[k, at, :], core, preferred_element_type=jnp.float32).astype(jnp.bfloat16)
            slab_ref[...] = slab_ref[...] - nt(part, u_ref[k])
            return 0

        lax.fori_loop(0, panels, panel, 0)
        waited(started([(tile_ref, out_hbm), (slab_ref, dout_hbm)], sems, 0))


def tile_scratch(panels, order, rank):
    stack = pltpu.VMEM((panels, order, rank), jnp.bfloat16)
    return [stack] * 4 + [pltpu.VMEM((order, order), jnp.float32), pltpu.VMEM((64, order), jnp.float32),
                          pltpu.SemaphoreType.DMA((130,)), pltpu.SemaphoreType.DMA((2 * panels,))]


def moved(value, pairs):
    return lax.ppermute(value, AXES, pairs)


def along(axis, change, parity):
    pairs = []
    for x in range(SIDE):
        for z in range(SIDE):
            for col in range(parity, 8, 2):
                to = (change(x), z) if axis == "x" else (x, change(z))
                pairs.append(((x * SIDE + z) * 8 + col, (to[0] * SIDE + to[1]) * 8 + col))
    return pairs


def across(change):
    return [(row * 8 + col, row * 8 + change(col)) for row in range(16) for col in range(8)]


def first_leg(a, b, parity):
    a, b = a[None], b[None]
    for change in (lambda p: p ^ 1, lambda p: p ^ 3):
        got_a = moved(a, along("x", change, parity))
        got_b = moved(b, along("z", change, parity))
        a, b = jnp.concatenate([a, got_a]), jnp.concatenate([b, got_b])
    return a, b


def second_leg(a, b, parity):
    got_a, got_b = [a, None, None, None], [b, None, None, None]
    for d in (1, 2, 3):
        got_a[d] = moved(a, along("z", lambda p: (p + d) % SIDE, parity))
        got_b[d] = moved(b, along("x", lambda p: (p + d) % SIDE, parity))
    return got_a, got_b


def shards(band, diag, row_factors, row_ranks, col_factors, col_ranks):
    column = lax.axis_index("cols")
    slab = lax.axis_index("rows")
    panels, slab_rows = col_factors.shape[0], diag.shape[1]
    order, rank = row_factors.shape[3], row_factors.shape[4]
    own_ranks = lax.dynamic_index_in_dim(col_ranks, column, 0, keepdims=False)
    meta = jnp.concatenate([jnp.stack([column, slab // SIDE, slab % SIDE, slab]).astype(jnp.int32), own_ranks])

    turned = row_factors[0, 0, 1].reshape(order // rank, rank, rank).transpose(0, 2, 1)
    kept = (jnp.arange(rank, dtype=jnp.int32) < row_ranks[0, 0])[None, :, None]
    turned = jnp.where(kept, turned, jnp.zeros((), turned.dtype)).reshape(order, rank)
    mine = jnp.stack([row_factors[0, 0, 0], turned])

    own = lax.all_to_all(col_factors, "cols", split_axis=0, concat_axis=1, tiled=True)[0]
    pieces = diag[0].reshape(slab_rows, 4, rank).transpose(1, 0, 2)
    rounded = lax.reduce_precision(pieces, exponent_bits=8, mantissa_bits=7)
    high = rounded.astype(jnp.bfloat16)
    low = (pieces - rounded).astype(jnp.bfloat16)
    own, mine, meta, high, low = lax.optimization_barrier((own, mine, meta, high, low))
    near = [mine]
    for d in (1, 2, 3):
        near.append(moved(mine, across(lambda c: ((c // 2 + d) % SIDE) * 2 + c % 2)))
    sides, bases = own[:, 1], own[:, 0]
    a, b = lax.optimization_barrier(first_leg(jnp.concatenate([sides, high]), jnp.concatenate([bases, low]), 0))
    fs, gs = second_leg(a, b, 0)
    far = [moved(p, across(lambda c: c ^ 1)) for p in near]
    odd_a, odd_b = first_leg(sides, bases, 1)
    seen = jnp.stack([fs[2][0, 0, :8, :128], gs[2][0, 0, :8, :128]])
    seen = lax.ppermute(seen, AXES, [(row * 8 + col, row * 8 + col + 1) for row in range(16) for col in range(0, 8, 2)])
    held = jnp.any(seen != seen)
    odd_a, odd_b, held = lax.optimization_barrier((odd_a, odd_b, held))
    odd_a, odd_b = [jnp.where(held, jnp.zeros((), p.dtype), p) for p in (odd_a, odd_b)]
    odd_fs, odd_gs = second_leg(odd_a, odd_b, 1)
    fs, gs, near, far, own_a, own_b = lax.optimization_barrier((fs, gs, near, far, odd_fs[0], odd_gs[0]))
    odd_fs, odd_gs = [own_a] + odd_fs[1:], [own_b] + odd_gs[1:]

    hbm = pl.BlockSpec(memory_space=pl.ANY)
    smem = pl.BlockSpec(memory_space=pltpu.SMEM)
    outs = (jax.ShapeDtypeStruct((order, order), jnp.float32), jax.ShapeDtypeStruct((slab_rows, order), jnp.float32))
    params = pltpu.CompilerParams(vmem_limit_bytes=COLUMN_GRANT)
    tile, slab_out = pl.pallas_call(
        column_kernel,
        out_shape=outs,
        in_specs=[smem] + [hbm] * 17,
        out_specs=(hbm, hbm),
        scratch_shapes=column_scratch(panels, order, rank),
        cost_estimate=pl.CostEstimate(flops=60_000_000_000, bytes_accessed=20_000_000, transcendentals=0),
        compiler_params=params, name="column")(meta, *fs, *gs, *near, *far, band[0, 0])

    tile, slab_out = pl.pallas_call(
        tile_kernel,
        out_shape=outs,
        in_specs=[smem] + [hbm] * 28,
        out_specs=(hbm, hbm),
        scratch_shapes=tile_scratch(panels, order, rank),
        input_output_aliases={27: 0, 28: 1},
        cost_estimate=pl.CostEstimate(flops=10_000_000_000, bytes_accessed=40_000_000, transcendentals=0),
        compiler_params=pltpu.CompilerParams(vmem_limit_bytes=TILE_GRANT), name="tile")(
            meta, *fs, *gs, *odd_fs, *odd_gs, *near, *far, band[0, 0], diag[0], tile, slab_out)
    return tile[None, None], slab_out[None]


def solution(mesh):
    placed = (
        P("rows", "cols", None, None),
        P("cols", "rows", None),
        P("rows", "cols", None, None, None),
        P("rows", "cols"),
        P(None, "cols", None, "rows", None),
        P(),
    )
    return jax.shard_map(
        shards,
        mesh=mesh,
        in_specs=placed,
        out_specs=(P("rows", "cols", None, None), P("cols", "rows", None)),
        check_vma=False,
    )
```

```python
import jax
import jax.numpy as jnp
from jax import lax
from jax.experimental import pallas as pl
from jax.experimental.pallas import tpu as pltpu
from jax.sharding import PartitionSpec as P


NB = 128
G = 8
SIDE = 4
AXES = ("rows", "cols")
NEAR = (0, 1, 3, 2)
GRANT = 46 << 20


def split2(x):
    hi = x.astype(jnp.bfloat16)
    lo = (x - hi.astype(jnp.float32)).astype(jnp.bfloat16)
    return hi, lo


def nt(a, b):
    return lax.dot_general(a, b, (((1,), (1,)), ((), ())), preferred_element_type=jnp.float32)


def nt3(ah, al, bh, bl):
    return nt(jnp.concatenate([ah, al, ah], axis=1), jnp.concatenate([bh, bh, bl], axis=1))


def lane_splat(x, lane):
    return jnp.broadcast_to(x[:, lane:lane + 1], x.shape)


def row_splat(x, s):
    return jnp.broadcast_to(x[s:s + 1, :], x.shape)


def factor_block(t_ref, up_ref, one_ref):
    one = one_ref[...]
    sub = lax.broadcasted_iota(jnp.int32, (G, NB), 0)
    lane = lax.broadcasted_iota(jnp.int32, (G, NB), 1)
    count = NB // G
    first = t_ref[0:G, :]
    diag = [lane_splat(first, c) * one for c in range(G)]
    for g in range(count):
        base = g * G
        v = t_ref[base:base + G, :]
        b = [[row_splat(diag[j], s) if s >= j else None for j in range(G)] for s in range(G)]
        more = g + 1 < count
        if more:
            below = t_ref[base + G:base + 2 * G, :]
            wn = [lane_splat(below, base + j) for j in range(G)]
            diag = [lane_splat(below, base + G + c) for c in range(G)]
        inside = (lane >= base) & (lane < base + G)
        vi = jnp.where(inside, jnp.where(lane - base == sub, 1.0, 0.0), v)
        low = [[None] * G for _ in range(G)]
        rinv = [None] * G
        ra = [row_splat(v, s) for s in range(G)]
        r = [row_splat(vi, s) for s in range(G)]
        for j in range(G):
            rinv[j] = lax.rsqrt(b[j][j])
            for s in range(j + 1, G):
                low[s][j] = b[s][j] * rinv[j]
            for t in range(j + 1, G):
                for s in range(t, G):
                    b[s][t] = b[s][t] - low[s][j] * low[t][j]
            if more:
                ln = wn[j] * rinv[j]
                for t in range(j + 1, G):
                    wn[t] = wn[t] - ln * low[t][j]
                for c in range(G):
                    diag[c] = diag[c] - ln * row_splat(ln, c)
            ra[j] = ra[j] * rinv[j]
            r[j] = r[j] * rinv[j]
            for s in range(j + 1, G):
                ra[s] = ra[s] - low[s][j] * ra[j]
                r[s] = r[s] - low[s][j] * r[j]
        out, outa = r[0], ra[0]
        for s in range(1, G):
            out = jnp.where(sub == s, r[s], out)
            outa = jnp.where(sub == s, ra[s], outa)
        up_ref[base:base + G, :] = outa
        t_ref[base:base + G, :] = out
        if more:
            m = [None] * G
            for s in reversed(range(G)):
                acc = r[s]
                for t in range(s + 1, G):
                    acc = acc - low[t][s] * m[t]
                m[s] = acc * rinv[s]
            for rb in range(g + 1, count):
                w = t_ref[rb * G:(rb + 1) * G, :]
                acc = jnp.where(inside, 0.0, w)
                for j in range(G):
                    acc = acc - lane_splat(w, base + j) * m[j]
                t_ref[rb * G:(rb + 1) * G, :] = acc


def chol_body(a_ref, inv_ref, t_ref, up_ref, one_ref, beside):
    n = a_ref.shape[0]
    nblk = n // NB
    ri = lax.broadcasted_iota(jnp.int32, (NB, NB), 0)
    ci = lax.broadcasted_iota(jnp.int32, (NB, NB), 1)

    def step(j, _):
        o = pl.multiple_of(j * NB, NB)
        t_ref[...] = a_ref[pl.ds(o, NB), pl.ds(o, NB)]
        factor_block(t_ref, up_ref, one_ref)
        beside(j)
        inv = jnp.where(ri >= ci, t_ref[...], 0.0)
        inv_ref[pl.ds(o, NB), :] = inv
        low = jnp.where(ri >= ci, up_ref[...].T, 0.0)
        ih, il = split2(inv)
        for v in range(nblk // 2):
            lo_row = 2 * NB * v

            @pl.when((j + 1) // 2 == v)
            def _():
                p = a_ref[lo_row:, pl.ds(o, NB)]
                ph, plo = split2(p)
                x = nt3(ph, plo, ih, il)
                rows = lax.broadcasted_iota(jnp.int32, x.shape, 0) + lo_row
                x = jnp.where(rows >= o + NB, x, 0.0)
                a_ref[lo_row:, pl.ds(o, NB)] = x
                xh, xl = split2(x)
                c = nt3(xh, xl, xh, xl)
                a_ref[lo_row:, lo_row:] = a_ref[lo_row:, lo_row:] - c
        a_ref[pl.ds(o, NB), pl.ds(o, NB)] = low
        return 0

    lax.fori_loop(0, nblk, step, 0)


def solve_body(b_ref, l_ref, inv_ref, x_ref, xh_ref, xl_ref, done):
    n = b_ref.shape[0]
    for j in range(n // (2 * NB)):
        o = 2 * NB * j
        s = slice(o, o + 2 * NB)
        i0, i1 = inv_ref[o:o + NB, :], inv_ref[o + NB:o + 2 * NB, :]
        i0h, i0l = split2(i0.T)
        i1h, i1l = split2(i1)
        mh, ml = split2(nt3(*split2(l_ref[o + NB:o + 2 * NB, o:o + NB]), i0h, i0l))
        off = -nt3(i1h, i1l, *split2(nt_same(mh, ml)))
        inv = jnp.concatenate([jnp.concatenate([i0, jnp.zeros_like(i0)], axis=1), jnp.concatenate([off, i1], axis=1)], axis=0)
        ih, il = split2(inv)
        acc = b_ref[:, s]
        if j:
            lh, ll = split2(l_ref[s, :o])
            acc = acc - nt(xh_ref[:, :o], lh) - nt(xl_ref[:, :o], lh) - nt(xh_ref[:, :o], ll)
        ah, al = split2(acc)
        x = nt3(ah, al, ih, il)
        x_ref[:, s] = x
        done(j, s)
        xh, xl = split2(x)
        xh_ref[:, s] = xh
        xl_ref[:, s] = xl


def nt_same(mh, ml):
    return (mh.astype(jnp.float32) + ml.astype(jnp.float32)).T


def tn(a, b):
    return lax.dot_general(a, b, (((0,), (0,)), ((), ())), preferred_element_type=jnp.float32)


def masked(core, rank_a, rank_b):
    kept = lax.broadcasted_iota(jnp.int32, core.shape, 1) < rank_b
    if rank_a is not None:
        kept = kept & (lax.broadcasted_iota(jnp.int32, core.shape, 0) < rank_a)
    return jnp.where(kept, core, 0.0).astype(jnp.bfloat16)


def started(pairs, sems, first=0):
    copies = [pltpu.make_async_copy(src, dst, sems.at[first + n]) for n, (src, dst) in enumerate(pairs)]
    for copy in copies:
        copy.start()
    return copies


def waited(copies):
    for copy in copies:
        copy.wait()


def slab_copies(meta, fs, gs, u_ref, v_ref, first, count, to=None):
    x, z = meta[1], meta[2]
    pairs = []
    for e in range(SIDE):
        for d in range(SIDE):
            for far, near, at_x, at_z, dst in (
                (e, d, x ^ NEAR[d], (z + SIDE - e) % SIDE, v_ref), (d, e, (x + SIDE - d) % SIDE, z ^ NEAR[e], u_ref)
            ):
                at = pl.ds(pl.multiple_of((at_x * SIDE + at_z) * 64, 64), 64)
                src = fs[far] if dst is v_ref else gs[far]
                pairs.append((src.at[near, pl.ds(first, count)], dst.at[pl.ds(first if to is None else to, count), at, :]))
    return pairs


def row_copies(meta, rows, ru_ref, rv_ref):
    y, core_at = meta[0] // 2, meta[0] % 2
    pairs = []
    for e in range(SIDE):
        near = ((y + SIDE - e) % SIDE) * 2
        for src, k in ((rows[e], near + core_at), (rows[SIDE + e], near + 1 - core_at)):
            pairs.append((src.at[0], ru_ref.at[k]))
            pairs.append((src.at[1], rv_ref.at[k]))
    return pairs


def tile_panel(meta, k, tile_ref, u_ref, v_ref, ru_ref, rv_ref):
    n = tile_ref.shape[0]
    core = jnp.dot(rv_ref[k, 0:256], v_ref[k, 0:256], preferred_element_type=jnp.float32)
    for q in range(256, n, 256):
        core = core + jnp.dot(rv_ref[k, q:q + 256], v_ref[k, q:q + 256], preferred_element_type=jnp.float32)
    core = masked(core, None, meta[4 + k])
    left = jnp.dot(ru_ref[k], core, preferred_element_type=jnp.float32).astype(jnp.bfloat16)
    uk = u_ref[k]
    for s in range(0, n, 512):
        tile_ref[s:s + 512, :] = tile_ref[s:s + 512, :] - nt(left[s:s + 512], uk)


def column_kernel(meta, fs, gs, rows, band_hbm, out_hbm, dout_hbm, u_ref, v_ref, ru_ref, rv_ref, tile_ref,
                  hi_ref, lo_ref, acc_ref, l_ref, inv_ref, t_ref, up_ref, one_ref, xh_ref, xl_ref, sems):
    n = l_ref.shape[0]

    @pl.when(meta[0] == 0)
    def _():
        one = started(slab_copies(meta, fs, gs, u_ref, v_ref, 0, 4), sems, 0)
        two = started(slab_copies(meta, fs, gs, u_ref, v_ref, 4, 4), sems, 32)
        three = started(slab_copies(meta, fs, gs, lo_ref, hi_ref, 8, 4, 0), sems, 64)
        acc_ref[...] = jnp.zeros_like(acc_ref)

        four = [pltpu.make_async_copy(src, dst, sems.at[96 + n])
                for n, (src, dst) in enumerate(row_copies(meta, rows, ru_ref, rv_ref) + [(band_hbm, tile_ref)])]

        def panel(k, _):
            @pl.when(k == 4)
            def _():
                waited(two)
                for copy in four:
                    copy.start()

            rank = meta[4 + k]
            vk, uk = v_ref[k], u_ref[k]
            core = masked(tn(vk, vk), rank, rank)
            left = jnp.dot(uk, core, preferred_element_type=jnp.float32).astype(jnp.bfloat16)
            for s in range(0, n, 512):
                acc_ref[s:s + 512, :] = acc_ref[s:s + 512, :] - nt(left[s:s + 512], uk)
            return 0

        waited(one)
        lax.fori_loop(0, 8, panel, 0, unroll=2)
        waited(three)

        def whole(rows, cols):
            q, at = cols.start // 256, slice(cols.start % 256, cols.start % 256 + NB)
            return acc_ref[rows, cols] + (hi_ref[q, rows, at].astype(jnp.float32) + lo_ref[q, rows, at].astype(jnp.float32))

        for i in range(n // NB):
            si = slice(i * NB, (i + 1) * NB)
            for j in range(i + 1):
                sj = slice(j * NB, (j + 1) * NB)
                l_ref[si, sj] = (whole(si, sj) + whole(sj, si).T) * 0.5
        waited(four)
        one_ref[...] = jnp.ones_like(one_ref)
        chol_body(l_ref, inv_ref, t_ref, up_ref, one_ref, lambda j: tile_panel(meta, j, tile_ref, u_ref, v_ref, ru_ref, rv_ref))
        for j in range(n // NB - 1):
            l_ref[j * NB:(j + 1) * NB, (j + 1) * NB:] = jnp.zeros((NB, n - (j + 1) * NB), jnp.float32)
        last = started([(l_ref.at[pl.ds(pl.multiple_of(meta[3] * 64, 64), 64), :], dout_hbm)], sems, 0)

        def done(j, s):
            last.extend(started([(tile_ref.at[:, s], out_hbm.at[:, s])], sems, 1 + j))

        solve_body(tile_ref, l_ref, inv_ref, tile_ref, xh_ref, xl_ref, done)
        waited(last)


def tile_kernel(meta, even, odd, rows, band_hbm, diag_hbm, out_hbm, dout_hbm, u_ref, v_ref, ru_ref, rv_ref, tile_ref, slab_ref, sems, row_sems):
    panels = u_ref.shape[0]
    at = pl.ds(pl.multiple_of(meta[3] * 64, 64), 64)
    y, core_at = meta[0] // 2, meta[0] % 2

    @pl.when(meta[0] != 0)
    def _():
        four = started([(band_hbm, tile_ref), (diag_hbm, slab_ref)], sems, 128)

        def start_columns(group, _):
            first = ((y + SIDE - group) % SIDE) * 2

            @pl.when(core_at == 0)
            def _():
                started(slab_copies(meta, even[:4], even[4:], u_ref, v_ref, first, 2), sems, 16 * first)

            @pl.when(core_at != 0)
            def _():
                started(slab_copies(meta, odd[:4], odd[4:], u_ref, v_ref, first, 2), sems, 16 * first)

            return 0

        for e in range(SIDE):
            near = ((y + SIDE - e) % SIDE) * 2
            for src, k in ((rows[e], near + core_at), (rows[SIDE + e], near + 1 - core_at)):
                pltpu.make_async_copy(src.at[0], ru_ref.at[k], row_sems.at[k]).start()
                pltpu.make_async_copy(src.at[1], rv_ref.at[k], row_sems.at[panels + k]).start()
        lax.fori_loop(0, panels // 2, start_columns, 0)
        waited(four)

        def panel(step, _):
            k = ((y + SIDE - step // 2) % SIDE) * 2 + step % 2

            @pl.when(k % 2 == 0)
            def _():
                waits = slab_copies(meta, odd[:4], odd[4:], u_ref, v_ref, k, 2)
                waited([pltpu.make_async_copy(src, dst, sems.at[16 * k + i]) for i, (src, dst) in enumerate(waits)])

            pltpu.make_async_copy(rows[0].at[0], ru_ref.at[k], row_sems.at[k]).wait()
            pltpu.make_async_copy(rows[0].at[1], rv_ref.at[k], row_sems.at[panels + k]).wait()
            tile_panel(meta, k, tile_ref, u_ref, v_ref, ru_ref, rv_ref)
            rank = meta[4 + k]
            vk = v_ref[k]
            core = masked(tn(vk, vk), rank, rank)
            part = jnp.dot(u_ref[k, at, :], core, preferred_element_type=jnp.float32).astype(jnp.bfloat16)
            slab_ref[...] = slab_ref[...] - nt(part, u_ref[k])
            return 0

        lax.fori_loop(0, panels, panel, 0, unroll=2)
        waited(started([(tile_ref, out_hbm), (slab_ref, dout_hbm)], sems, 0))


def device_kernel(meta, *refs):
    even, odd, rows = refs[0:8], refs[8:16], refs[16:24]
    band_hbm, diag_hbm, out_hbm, dout_hbm = refs[24:28]
    shared, slab_ref, own, sems, row_sems = refs[28:33], refs[33], refs[34:-2], refs[-2], refs[-1]
    column_kernel(meta, even[:4], even[4:], rows, band_hbm, out_hbm, dout_hbm, *shared, *own, sems)
    tile_kernel(meta, even, odd, rows, band_hbm, diag_hbm, out_hbm, dout_hbm, *shared, slab_ref, sems, row_sems)


def device_scratch(panels, order, rank):
    stack = pltpu.VMEM((panels, order, rank), jnp.bfloat16)
    quarter = pltpu.VMEM((4, order, rank), jnp.bfloat16)
    square = pltpu.VMEM((order, order), jnp.float32)
    block = pltpu.VMEM((NB, NB), jnp.float32)
    return [stack] * 4 + [square, pltpu.VMEM((64, order), jnp.float32), quarter, quarter, square, square,
            pltpu.VMEM((order, NB), jnp.float32), block, block, pltpu.VMEM((G, NB), jnp.float32),
            pltpu.VMEM((order, order), jnp.bfloat16), pltpu.VMEM((order, order), jnp.bfloat16),
            pltpu.SemaphoreType.DMA((130,)), pltpu.SemaphoreType.DMA((2 * panels,))]


def moved(value, pairs):
    return lax.ppermute(value, AXES, pairs)


def along(axis, change, parity):
    pairs = []
    for x in range(SIDE):
        for z in range(SIDE):
            for col in range(parity, 8, 2):
                to = (change(x), z) if axis == "x" else (x, change(z))
                pairs.append(((x * SIDE + z) * 8 + col, (to[0] * SIDE + to[1]) * 8 + col))
    return pairs


def across(change):
    return [(row * 8 + col, row * 8 + change(col)) for row in range(16) for col in range(8)]


def first_leg(a, b, parity):
    a, b = a[None], b[None]
    for change in (lambda p: p ^ 1, lambda p: p ^ 3):
        got_a = moved(a, along("x", change, parity))
        got_b = moved(b, along("z", change, parity))
        a, b = jnp.concatenate([a, got_a]), jnp.concatenate([b, got_b])
    return a, b


def second_leg(a, b, parity):
    got_a, got_b = [a, None, None, None], [b, None, None, None]
    for d in (1, 2, 3):
        got_a[d] = moved(a, along("z", lambda p: (p + d) % SIDE, parity))
        got_b[d] = moved(b, along("x", lambda p: (p + d) % SIDE, parity))
    return got_a, got_b


def shards(band, diag, row_factors, row_ranks, col_factors, col_ranks):
    column = lax.axis_index("cols")
    slab = lax.axis_index("rows")
    panels, slab_rows = col_factors.shape[0], diag.shape[1]
    order, rank = row_factors.shape[3], row_factors.shape[4]
    own_ranks = lax.dynamic_index_in_dim(col_ranks, column, 0, keepdims=False)
    meta = jnp.concatenate([jnp.stack([column, slab // SIDE, slab % SIDE, slab]).astype(jnp.int32), own_ranks])

    turned = row_factors[0, 0, 1].reshape(order // rank, rank, rank).transpose(0, 2, 1)
    kept = (jnp.arange(rank, dtype=jnp.int32) < row_ranks[0, 0])[None, :, None]
    turned = jnp.where(kept, turned, jnp.zeros((), turned.dtype)).reshape(order, rank)
    mine = jnp.stack([row_factors[0, 0, 0], turned])

    own = lax.all_to_all(col_factors, "cols", split_axis=0, concat_axis=1, tiled=True)[0]
    pieces = diag[0].reshape(slab_rows, 4, rank).transpose(1, 0, 2)
    rounded = lax.reduce_precision(pieces, exponent_bits=8, mantissa_bits=7)
    high = rounded.astype(jnp.bfloat16)
    low = (pieces - rounded).astype(jnp.bfloat16)
    own, mine, meta, high, low = lax.optimization_barrier((own, mine, meta, high, low))
    near = [mine]
    for d in (1, 2, 3):
        near.append(moved(mine, across(lambda c: ((c // 2 + d) % SIDE) * 2 + c % 2)))
    sides, bases = own[:, 1], own[:, 0]
    a, b = lax.optimization_barrier(first_leg(jnp.concatenate([sides, high]), jnp.concatenate([bases, low]), 0))
    fs, gs = second_leg(a, b, 0)
    far = [moved(p, across(lambda c: c ^ 1)) for p in near]
    odd_a, odd_b = lax.optimization_barrier(first_leg(sides, bases, 1))
    odd_fs, odd_gs = second_leg(odd_a, odd_b, 1)
    fs, gs, near, far, own_a, own_b = lax.optimization_barrier((fs, gs, near, far, odd_fs[0], odd_gs[0]))
    odd_fs, odd_gs = [own_a] + odd_fs[1:], [own_b] + odd_gs[1:]

    hbm = pl.BlockSpec(memory_space=pl.ANY)
    smem = pl.BlockSpec(memory_space=pltpu.SMEM)
    outs = (jax.ShapeDtypeStruct((order, order), jnp.float32), jax.ShapeDtypeStruct((slab_rows, order), jnp.float32))
    tile, slab_out = pl.pallas_call(
        device_kernel,
        out_shape=outs,
        in_specs=[smem] + [hbm] * 26,
        out_specs=(hbm, hbm),
        scratch_shapes=device_scratch(panels, order, rank),
        cost_estimate=pl.CostEstimate(flops=60_000_000_000, bytes_accessed=40_000_000, transcendentals=0),
        compiler_params=pltpu.CompilerParams(vmem_limit_bytes=GRANT), name="device")(
            meta, *fs, *gs, *odd_fs, *odd_gs, *near, *far, band[0, 0], diag[0])
    return tile[None, None], slab_out[None]


def solution(mesh):
    placed = (
        P("rows", "cols", None, None),
        P("cols", "rows", None),
        P("rows", "cols", None, None, None),
        P("rows", "cols"),
        P(None, "cols", None, "rows", None),
        P(),
    )
    return jax.shard_map(
        shards,
        mesh=mesh,
        in_specs=placed,
        out_specs=(P("rows", "cols", None, None), P("cols", "rows", None)),
        check_vma=False,
    )
```
